128 devices in a mesh: item: 4 (over z), user: 32 (over y, x, core).
Axes of the slice: x: 4, y: 4, z: 4, core: 2. Of those that a mesh axis runs over, the one named last changes fastest.
Arguments:
- interactions: bfloat16 [65536, 16384], P('user', 'item'), may hold values from 0 to 1, as said below
- omega: float32 [16384, 256], P('item'), may hold values from -6 to 6
Outputs:
- scaled_basis: float32 [16384, 256], P('item')
The draws below stay inside these ranges and needn't reach their ends.
Inputs may be any that keep to these rules, and one draw needn't show every extreme that they name: `interactions`: every entry is 0 or 1.
All inputs are finite; a program needn't handle non-finite values.
Results may differ from the reference program's by a relative error of at most 0.0003.
Values sent between devices are 32-bit elements; how exact they have to be, the bound alone decides.
No kernel may reach another device: no remote copies, remote signals or barrier semaphores. Data moves between devices by JAX's collectives and lax.ppermute only.
A program may use at most 128 MiB of HBM per device.

```python
import jax
import jax.numpy as jnp
from jax import lax

RANK = 256
U_DEV = 2048
USERS = 65536
ITEMS = 16384
N_USER = 32


def draw_interactions(key, part):
    first, second, third = jax.random.split(key, 3)
    activity = jnp.exp(jax.random.uniform(first, (USERS, 1), jnp.float32, jnp.log(0.01), jnp.log(0.15)))
    popularity = jnp.exp(jax.random.uniform(second, (1, ITEMS), jnp.float32, jnp.log(0.3), jnp.log(8.0)))
    chance = jnp.minimum(activity * popularity, 1.0)
    touched = jax.random.uniform(third, (USERS, ITEMS), jnp.float32) < chance
    return touched.astype(jnp.float32).astype(jnp.bfloat16)


def levels(own_key, extent, shards, low, top_value):
    gain, own = 1.0, jax.random.fold_in(own_key, 6)
    for axis_at, shards_of in shards:
        draws = jnp.exp(jax.random.uniform(jax.random.fold_in(own, axis_at), (shards_of,), jnp.float32, low / len(shards), top_value / len(shards)))
        gain = gain * jnp.repeat(draws, extent[axis_at] // shards_of).reshape([-1 if axis == axis_at else 1 for axis in range(len(extent))])
    return gain


def centred(rng, shape, spread, reach, shards=(), dtype=jnp.bfloat16):
    entries = spread * jax.random.normal(rng, shape, jnp.float32)
    if shards:
        entries = entries * levels(rng, shape, shards, -0.22, 0.18)
    return jnp.clip(entries, -reach, reach).astype(dtype)


def setup_inputs(seed: int = 0) -> dict:
    key_of = jax.random.split(jax.random.key(seed), 3)
    return {
        "interactions": draw_interactions(jax.random.fold_in(key_of[2], 71), 0),
        "omega": centred(key_of[1], (ITEMS, RANK), 1.0, 6.0, ((0, 4),), jnp.float32),
    }


ridge = 200.0
highest = lax.Precision.HIGHEST

def orthonormal(block):
    gram = lax.dot_general(block.astype(jnp.float32), block.astype(jnp.float32), (((0,), (0,)), ((), ())), precision=highest, preferred_element_type=jnp.float32)
    lower = jnp.linalg.cholesky(gram)
    return lax.linalg.triangular_solve(lower, block, left_side=False, lower=True, transpose_a=True)

def reference(interactions, omega):
    slabs = interactions.reshape(N_USER, U_DEV, ITEMS)

    def add_slab(total, slab):
        slab = slab.astype(jnp.float32)
        rows = jnp.dot(slab.astype(jnp.float32), omega.astype(jnp.float32), precision=highest, preferred_element_type=jnp.float32)
        term = lax.dot_general(slab.astype(jnp.float32), rows.astype(jnp.float32), (((0,), (0,)), ((), ())), precision=highest, preferred_element_type=jnp.float32)
        return (total + term, None)
    sketch, unused = lax.scan(add_slab, jnp.zeros((ITEMS, RANK), jnp.float32), slabs)
    sketch = sketch + ridge * omega
    basis = orthonormal(orthonormal(sketch))
    return jnp.sqrt(jnp.float32(ITEMS)) * basis
```

```python
import jax
import jax.numpy as jnp
from jax import lax
from jax.experimental import pallas as pl
from jax.experimental.pallas import tpu as pltpu
from jax.sharding import PartitionSpec as P

ridge = 200.0
highest = lax.Precision.HIGHEST
f32 = jnp.float32
bf16 = jnp.bfloat16
side = 4
steps = (1, 3, 2)


def exact_dot(a, b, ca, cb):
    return lax.dot_general(a, b, (((ca,), (cb,)), ((), ())), precision=highest, preferred_element_type=f32)


def fast_dot(a, b):
    return lax.dot_general(a, b, (((1,), (0,)), ((), ())), preferred_element_type=f32)


def slices(x):
    high = x.astype(bf16)
    return high, (x - high.astype(f32)).astype(bf16)


def perm_of(axis, step):
    stride, size = {"y": (8, 4), "x": (2, 4), "core": (1, 2)}[axis]
    pairs = []
    for u in range(32):
        at = u // stride % size
        pairs.append((u, u + ((at + step) % size - at) * stride))
    return pairs


def shift(a, axis, step):
    if axis == "item":
        return lax.ppermute(a, "item", [(i, (i + step) % side) for i in range(side)])
    return lax.ppermute(a, "user", perm_of(axis, step))


def rows_kernel(a_ref, omega_ref, y_ref, high, low):
    @pl.when(pl.program_id(0) == 0)
    def _():
        high[...], low[...] = slices(omega_ref[...])

    a = a_ref[...]
    y_ref[...] = fast_dot(a, high[...]) + fast_dot(a, low[...])


def user_rows(a, omega, block=512):
    users, items = a.shape
    rank = omega.shape[1]
    return pl.pallas_call(
        rows_kernel,
        out_shape=jax.ShapeDtypeStruct((users, rank), f32),
        grid=(users // block,),
        in_specs=[
            pl.BlockSpec((block, items), lambda i: (i, 0)),
            pl.BlockSpec((items, rank), lambda i: (0, 0), pipeline_mode=pl.Buffered(1)),
        ],
        out_specs=pl.BlockSpec((block, rank), lambda i: (i, 0)),
        scratch_shapes=[pltpu.VMEM((items, rank), bf16)] * 2,
        name="user_rows",
    )(a, omega)


def columns_kernel(place_ref, y0, y1, y2, y3, a_ref, z_ref, both):
    rank = y0.shape[0]
    span = y0.shape[1]

    @pl.when(pl.program_id(0) == 0)
    def _():
        for d, ref in enumerate((y0, y1, y2, y3)):
            at = pl.ds(pl.multiple_of(place_ref[d] * span, span), span)
            both[:rank, at], both[rank:, at] = slices(ref[...])

    out = fast_dot(both[...], a_ref[...])
    z = out[:rank] + out[rank:]
    z_ref[0, 0] = z[: rank // 2]
    z_ref[0, 1] = z[rank // 2 :]


def item_columns(place, ys, a, half, block=512):
    users, items = a.shape
    rank = ys[0].shape[0]
    count = items // 2 // block
    whole = pl.BlockSpec(ys[0].shape, lambda i, s: (0, 0), pipeline_mode=pl.Buffered(1))
    return pl.pallas_call(
        columns_kernel,
        out_shape=jax.ShapeDtypeStruct((count, 2, rank // 2, block), f32),
        grid_spec=pltpu.PrefetchScalarGridSpec(
            num_scalar_prefetch=1,
            grid=(count,),
            in_specs=[whole] * 4 + [pl.BlockSpec((users, block), lambda i, s: (0, s[4] * count + i))],
            out_specs=pl.BlockSpec((1, 2, rank // 2, block), lambda i, s: (i, 0, 0, 0)),
            scratch_shapes=[pltpu.VMEM((2 * rank, users), bf16)],
        ),
        name="item_columns",
    )(jnp.concatenate([place, half.reshape(1)]), *ys, a)


def inverse_factor_half(block):
    n = block.shape[0]
    count = n // 8
    lanes = lax.broadcasted_iota(jnp.int32, (8, n), 1)
    subs = lax.broadcasted_iota(jnp.int32, (8, n), 0)
    rows = [block[8 * k : 8 * k + 8, :] for k in range(count)]
    pivots = []
    for j in range(n):
        b, s = divmod(j, 8)
        at = lanes == j
        lead = rows[b][s : s + 1, :]
        pivot = lead[:, j : j + 1]
        pivots.append(pivot)
        lead = jnp.broadcast_to(jnp.where(at[:1], 1.0, lead) * (1.0 / pivot), (8, n))
        for k in range(b, count):
            column = jnp.broadcast_to(rows[k][:, j : j + 1], (8, n))
            new = jnp.where(at, 0.0, rows[k]) - column * lead
            if k == b:
                new = jnp.where(subs > s, new, jnp.where(at & (subs == s), 1.0, rows[k]))
            rows[k] = new
    out = []
    for k in range(count):
        pivot = jnp.concatenate(pivots[8 * k : 8 * k + 8], axis=0)
        out.append(jnp.where(lanes <= subs + 8 * k, rows[k], 0.0) * lax.rsqrt(pivot))
    return jnp.concatenate(out, axis=0)


def inverse_factor(gram):
    h = gram.shape[0] // 2
    first = inverse_factor_half(gram[:h, :h])
    below = exact_dot(gram[h:, :h], first, 1, 1)
    second = inverse_factor_half(gram[h:, h:] - exact_dot(below, below, 1, 1))
    mixed = -exact_dot(second, exact_dot(below, first, 1, 0), 1, 0)
    top = jnp.concatenate([first, jnp.zeros_like(first)], axis=1)
    return jnp.concatenate([top, jnp.concatenate([mixed, second], axis=1)], axis=0)


def pieces(refs, place_ref, at, count):
    own_l, own_r, far_l, far_r = refs
    out = []
    for half, (own, far) in enumerate(((own_l, far_l), (own_r, far_r))):
        row = []
        for k in range(count):
            ref = own if at < 16 else far
            row.append(ref[place_ref[half * 16 + (at + k) % 16]])
        out.append(jnp.concatenate(row, axis=1))
    return jnp.concatenate(out, axis=0)


def gram_kernel(place_ref, own_l, own_r, far_l, far_r, s_ref, g_ref):
    total = None
    for at in range(0, 32, 4):
        block = pieces((own_l, own_r, far_l, far_r), place_ref, at, 4)
        s_ref[:, at * 128 : at * 128 + 512] = block
        term = exact_dot(block, block, 1, 1)
        total = term if total is None else total + term
    g_ref[...] = total


def first_gram(place, parts):
    rank = 2 * parts[0].shape[1]
    vmem = pl.BlockSpec(memory_space=pltpu.VMEM)
    return pl.pallas_call(
        gram_kernel,
        out_shape=(jax.ShapeDtypeStruct((rank, 4096), f32), jax.ShapeDtypeStruct((rank, rank), f32)),
        in_specs=[pl.BlockSpec(memory_space=pltpu.SMEM)] + [vmem] * 4,
        out_specs=(vmem, vmem),
        name="first_gram",
    )(place, *parts)


def first_kernel(s_ref, g_ref, b_ref, g2_ref):
    inverse = inverse_factor(g_ref[...])
    total = None
    for at in range(0, s_ref.shape[1], 512):
        block = exact_dot(inverse, s_ref[:, at : at + 512], 1, 0)
        b_ref[:, at : at + 512] = block
        term = exact_dot(block, block, 1, 1)
        total = term if total is None else total + term
    g2_ref[...] = total


def first_sweep(s, gram):
    vmem = pl.BlockSpec(memory_space=pltpu.VMEM)
    return pl.pallas_call(
        first_kernel,
        out_shape=(jax.ShapeDtypeStruct(s.shape, f32), jax.ShapeDtypeStruct(gram.shape, f32)),
        in_specs=[vmem] * 2,
        out_specs=(vmem, vmem),
        name="first_sweep",
    )(s, gram)


def second_kernel(scale, order_ref, b_ref, g_ref, out_ref, inverse):
    @pl.when(pl.program_id(0) == 0)
    def _():
        inverse[...] = inverse_factor(g_ref[...])

    out_ref[...] = exact_dot(inverse[...], b_ref[...], 1, 0).T * scale


def second_sweep(half, b, gram, scale, block=512):
    rank, items = b.shape
    count = items // block
    return pl.pallas_call(
        lambda *refs: second_kernel(scale, *refs),
        out_shape=jax.ShapeDtypeStruct((items, rank), f32),
        grid_spec=pltpu.PrefetchScalarGridSpec(
            num_scalar_prefetch=1,
            grid=(count,),
            in_specs=[
                pl.BlockSpec((rank, block), lambda i, h: (0, i)),
                pl.BlockSpec((rank, rank), lambda i, h: (0, 0), pipeline_mode=pl.Buffered(1)),
            ],
            out_specs=pl.BlockSpec((block, rank), lambda i, h: ((i + h[0] * (count // 2)) % count, 0)),
            scratch_shapes=[pltpu.VMEM((rank, rank), f32)],
        ),
        name="second_sweep",
    )(half, b, gram)


def local(interactions, omega):
    user = lax.axis_index("user")
    z, core, x, y = lax.axis_index("item"), user % 2, user // 2 % side, user // 8
    users = interactions.shape[0]
    rank = omega.shape[1]
    half = rank // 2
    item_count = omega.shape[0] * lax.axis_size("item")

    rows = user_rows(interactions, omega)
    span = users // side
    quarter = lambda d: lax.dynamic_slice_in_dim(rows, (z + d) % side * span, span, 0)
    got = [shift(quarter(d), "item", d) for d in steps]
    own = (quarter(0) + got[0] + got[1] + got[2]).T
    ys = [own] + [shift(own, "item", d) for d in steps]
    place = jnp.stack([(z - d) % side for d in (0, *steps)])

    away = shift(item_columns(place, ys, interactions, 1 - core), "core", 1)
    kept = item_columns(place, ys, interactions, core) + away

    def scatter(parts, axis, at):
        got = [shift(parts((at + d) % side), axis, d) for d in steps]
        return parts(at) + got[0] + got[1] + got[2]

    def first_part(lane):
        return lambda k: lax.dynamic_slice(kept, (k, lane, 0, 0), (1, 1, half, 512))[0, 0]

    def later_part(block):
        return lambda k: lax.dynamic_slice_in_dim(block, k * 128, 128, 1)

    left = scatter(first_part(0), "x", x)
    right = scatter(first_part(1), "y", y)
    left = scatter(later_part(left), "y", y)
    right = scatter(later_part(right), "x", x)
    omega_left = lax.dynamic_slice(omega, (core * 2048 + x * 512 + y * 128, 0), (128, half))
    omega_right = lax.dynamic_slice(omega, (core * 2048 + y * 512 + x * 128, half), (128, half))
    left = left + ridge * omega_left.T
    right = right + ridge * omega_right.T

    def gather(block, axis):
        return jnp.stack([block] + [shift(block, axis, d) for d in steps])

    left = gather(gather(left, "y"), "x").reshape(16, half, 128)
    right = gather(gather(right, "x"), "y").reshape(16, half, 128)
    parts = (left, right, shift(left, "core", 1), shift(right, "core", 1))
    slot = jnp.asarray([0, 1, 3, 2])
    offs = jnp.arange(side)
    near = lambda at: slot[(at - offs) % side]
    table = jnp.concatenate(
        [
            (near(x)[:, None] * side + near(y)[None, :]).reshape(16),
            (near(y)[:, None] * side + near(x)[None, :]).reshape(16),
        ]
    ).astype(jnp.int32)
    s, gram = first_gram(table, parts)

    def over_items(g):
        h = g.shape[0] // 2
        mine = lax.dynamic_slice_in_dim(g, core * h, h, 0)
        got = [shift(mine, "item", d) for d in steps]
        terms = jnp.stack([mine, *got])
        mine = sum(lax.dynamic_index_in_dim(terms, slot[(z - k) % side], 0, False) for k in range(side))
        other = shift(mine, "core", 1)
        low = jnp.where(core == 0, mine, other)
        high = jnp.where(core == 0, other, mine)
        return jnp.concatenate([low, high], axis=0)

    basis, gram = first_sweep(s, over_items(gram))
    scale = float(item_count) ** 0.5
    return second_sweep(core.reshape(1).astype(jnp.int32), basis, over_items(gram), scale)


def solution(mesh):
    in_specs = (P("user", "item"), P("item", None))
    out_specs = P("item", None)
    return jax.shard_map(local, mesh=mesh, in_specs=in_specs, out_specs=out_specs, check_vma=False)
```

```python
import jax
import jax.numpy as jnp
from jax import lax
from jax.experimental import pallas as pl
from jax.experimental.pallas import tpu as pltpu
from jax.sharding import PartitionSpec as P

ridge = 200.0
highest = lax.Precision.HIGHEST
f32 = jnp.float32
bf16 = jnp.bfloat16
side = 4
steps = (1, 3, 2)
piece = 128


def exact_dot(a, b, ca, cb):
    return lax.dot_general(a, b, (((ca,), (cb,)), ((), ())), precision=highest, preferred_element_type=f32)


def fast_dot(a, b):
    return lax.dot_general(a, b, (((1,), (0,)), ((), ())), preferred_element_type=f32)


def slices(x):
    high = x.astype(bf16)
    return high, (x - high.astype(f32)).astype(bf16)


def pairs_of(axis, step):
    pairs = []
    for u in range(2 * side * side):
        y, x, core = u // (2 * side), u // 2 % side, u % 2
        if axis == "core":
            core = 1 - core
        elif (axis == "first") == (core == 0):
            x = (x + step) % side
        else:
            y = (y + step) % side
        pairs.append((u, (y * side + x) * 2 + core))
    return pairs


def shift(a, axis, step=1):
    if axis == "item":
        return lax.ppermute(a, "item", [(i, (i + step) % side) for i in range(side)])
    return lax.ppermute(a, "user", pairs_of(axis, step))


def first_rows_kernel(place_ref, a_ref, omega_ref, y_ref, high_ref, low_ref):
    high, low = slices(omega_ref[...])
    high_ref[...], low_ref[...] = high, low
    a = a_ref[...]
    y = fast_dot(a, high) + fast_dot(a, low)

    @pl.when(pl.program_id(0) == 0)
    def _():
        y_ref[...] = y

    @pl.when(pl.program_id(0) > 0)
    def _():
        y_ref[...] += y


def rows_kernel(place_ref, a_ref, high_ref, low_ref, y_ref):
    a = a_ref[...]
    y = fast_dot(a, high_ref[...]) + fast_dot(a, low_ref[...])

    @pl.when(pl.program_id(0) == 0)
    def _():
        y_ref[...] = y

    @pl.when(pl.program_id(0) > 0)
    def _():
        y_ref[...] += y


def user_rows(at, a, *omega, depth=1024):
    users, items = a.shape
    span = users // side
    rank = omega[0].shape[1]
    right = pl.BlockSpec((depth, rank), lambda k, s: (k, 0))
    out_spec = pl.BlockSpec((span, rank), lambda k, s: (0, 0))
    out_shape = jax.ShapeDtypeStruct((span, rank), f32)
    first = len(omega) == 1
    if first:
        out_spec = (out_spec, right, right)
        out_shape = (out_shape,) + (jax.ShapeDtypeStruct((items, rank), bf16),) * 2
    return pl.pallas_call(
        first_rows_kernel if first else rows_kernel,
        out_shape=out_shape,
        grid_spec=pltpu.PrefetchScalarGridSpec(
            num_scalar_prefetch=1,
            grid=(items // depth,),
            in_specs=[pl.BlockSpec((span, depth), lambda k, s: (s[0], k))] + [right] * len(omega),
            out_specs=out_spec,
        ),
        name="user_rows",
    )(at.reshape(1).astype(jnp.int32), a, *omega)


def columns_kernel(count, adds, place_ref, *refs):
    ys, blocks = refs[:count], refs[count : 2 * count]
    z_ref, both = refs[-2], refs[-1]
    rank, span = ys[0].shape

    @pl.when(pl.program_id(0) == 0)
    def _():
        for d, ref in enumerate(ys):
            both[:rank, d * span : d * span + span], both[rank:, d * span : d * span + span] = slices(ref[...])

    out = None
    for d, ref in enumerate(blocks):
        term = fast_dot(both[:, d * span : d * span + span], ref[...])
        out = term if out is None else out + term
    z = out[:rank] + out[rank:]
    width = z_ref.shape[2]
    for k in range(z_ref.shape[0]):
        part = z[:, k * width : k * width + width]
        z_ref[k] = part + refs[2 * count][k] if adds else part


def item_columns(place, ys, a, total=None, only=None, block=1024):
    users, items = a.shape
    rank, span = ys[0].shape
    count = len(ys)
    width = items // 8
    per = block // width
    grid = items // block // (1 if only is None else 2)
    start = 0 if not only else grid
    in_half = items // block // 2

    def of_items(i, s):
        at = i + start
        core = s[count]
        return (at // in_half + 1 + core) % 2 * in_half + at % in_half

    ins = [pl.BlockSpec((rank, span), lambda i, s: (0, 0), pipeline_mode=pl.Buffered(1))] * count
    for d in range(count):
        ins.append(pl.BlockSpec((span, block), lambda i, s, d=d: (s[d], of_items(i, s))))
    args = [*ys, *[a] * count]
    if total is not None:
        ins.append(pl.BlockSpec((per, rank, width), lambda i, s: (i + start, 0, 0)))
        args.append(total)
    return pl.pallas_call(
        lambda *refs: columns_kernel(count, total is not None, *refs),
        out_shape=jax.ShapeDtypeStruct((grid * per, rank, width), f32),
        grid_spec=pltpu.PrefetchScalarGridSpec(
            num_scalar_prefetch=1,
            grid=(grid,),
            in_specs=ins,
            out_specs=pl.BlockSpec((per, rank, width), lambda i, s: (i, 0, 0)),
            scratch_shapes=[pltpu.VMEM((2 * rank, count * span), bf16)],
        ),
        name="item_columns",
    )(place, *args)


def inverse_factor_half(block):
    n = block.shape[0]
    count = n // 8
    tile = (8, n)
    lanes = lax.broadcasted_iota(jnp.int32, tile, 1)
    subs = lax.broadcasted_iota(jnp.int32, tile, 0)
    spread = lambda v: jnp.broadcast_to(v, tile)
    rows = [block[8 * k : 8 * k + 8, :] for k in range(count)]
    out = []
    for p in range(count):
        c = 8 * p
        panel = rows[p]
        mine = [spread(panel[:, c + t : c + t + 1]) for t in range(8)]
        invs, leads, tops, scale = [], [], [], jnp.ones(tile, f32)
        for j in range(8):
            pivot = spread(mine[j][j : j + 1, :])
            inv = 1.0 / pivot
            invs.append(inv)
            scale = jnp.where(subs == j, pivot, scale)
            factor = jnp.where(subs > j, mine[j] * inv, 0.0)
            tops.append([None] * (j + 1) + [spread(mine[t][j : j + 1, :]) for t in range(j + 1, 8)])
            for t in range(j + 1, 8):
                mine[t] = mine[t] - factor * tops[j][t]
            panel = jnp.where((lanes == c + j) & (subs >= j), jnp.where(subs == j, 1.0, 0.0), panel)
            lead = spread(panel[j : j + 1, :])
            panel = panel - factor * lead
            leads.append(jnp.where((lanes > c + j) & (lanes < c + 8), 0.0, lead))
        out.append(jnp.where(lanes <= subs + c, panel, 0.0) * lax.rsqrt(scale))
        cleared = (lanes >= c) & (lanes < c + 8)
        for k in range(p + 1, count):
            his = [spread(rows[k][:, c + t : c + t + 1]) for t in range(8)]
            new = jnp.where(cleared, 0.0, rows[k])
            for j in range(8):
                factor = his[j] * invs[j]
                for t in range(j + 1, 8):
                    his[t] = his[t] - factor * tops[j][t]
                new = new - factor * leads[j]
            rows[k] = new
    return jnp.concatenate(out, axis=0)


def inverse_factor(gram, out, block, firsts, belows):
    h = block.shape[0]
    block[...] = gram[:h, :h]

    def half(i, carry):
        first = inverse_factor_half(block[...])
        below = exact_dot(gram[h:, :h], first, 1, 1)
        firsts[i] = first
        belows[i] = below
        block[...] = gram[h:, h:] - exact_dot(below, below, 1, 1)
        return carry

    lax.fori_loop(0, 2, half, 0)
    out[:h, :h] = firsts[0]
    out[:h, h:] = jnp.zeros((h, h), f32)
    out[h:, :h] = -exact_dot(firsts[1], exact_dot(belows[0], firsts[0], 1, 0), 1, 0)
    out[h:, h:] = firsts[1]


def factor_scratch(rank):
    h = rank // 2
    return [pltpu.VMEM(shape, f32) for shape in ((rank, rank), (h, h), (2, h, h), (2, h, h))]


def part_of(order_ref, ref, half):
    return jnp.concatenate([ref[order_ref[half * 4 + k]] for k in range(4)], axis=1)


def in_order(order_ref, grams):
    total = None
    for h in range(2):
        half = (order_ref[16] + h) % 2
        for k in range(4):
            term = grams[half * 4 + order_ref[8 + half * 4 + k]]
            total = term if total is None else total + term
    return total


def some_grams_kernel(order_ref, *refs):
    out = refs[-1]
    for k, ref in enumerate(refs[:-1]):
        part = part_of(order_ref, ref, k // 3)
        out[k // 3 * 4 + k % 3] = exact_dot(part, part, 1, 1)


def gram_kernel(order_ref, near_ref, far_ref, some_ref, out_ref, grams):
    for half, ref in enumerate((near_ref, far_ref)):
        grams[half * 4 : half * 4 + 3] = some_ref[half * 4 : half * 4 + 3]
        part = part_of(order_ref, ref, half)
        grams[half * 4 + 3] = exact_dot(part, part, 1, 1)
    out_ref[...] = in_order(order_ref, grams)


vmem = pl.BlockSpec(memory_space=pltpu.VMEM)
smem = pl.BlockSpec(memory_space=pltpu.SMEM)


def first_gram(order, near, far):
    rank = near[0].shape[1]
    some = pl.pallas_call(
        some_grams_kernel,
        out_shape=jax.ShapeDtypeStruct((8, rank, rank), f32),
        in_specs=[smem] + [vmem] * 6,
        out_specs=vmem,
        name="some_grams",
    )(order, *near[:3], *far[:3])
    return pl.pallas_call(
        gram_kernel,
        out_shape=jax.ShapeDtypeStruct((rank, rank), f32),
        in_specs=[smem] + [vmem] * 3,
        out_specs=vmem,
        scratch_shapes=[pltpu.VMEM((8, rank, rank), f32)],
        name="first_gram",
    )(order, near[3], far[3], some)


def first_kernel(order_ref, gram_ref, *refs):
    parts, (basis_ref, out_ref, grams, inverse), scratch = refs[:8], refs[8:12], refs[12:]
    inverse_factor(gram_ref, inverse, *scratch)
    for k, ref in enumerate(parts):
        block = exact_dot(inverse[...], part_of(order_ref, ref, k // 4), 1, 0)
        basis_ref[k] = block
        grams[k] = exact_dot(block, block, 1, 1)
    out_ref[...] = in_order(order_ref, grams)


def first_sweep(order, gram, parts):
    rank = gram.shape[0]
    return pl.pallas_call(
        first_kernel,
        out_shape=(jax.ShapeDtypeStruct((8, rank, 4 * piece), f32), jax.ShapeDtypeStruct((rank, rank), f32)),
        in_specs=[smem] + [vmem] * 9,
        out_specs=(vmem, vmem),
        scratch_shapes=[pltpu.VMEM((8, rank, rank), f32)] + factor_scratch(rank),
        name="first_sweep",
    )(order, gram, *parts)


def second_kernel(scale, place_ref, basis_ref, gram_ref, out_ref, inverse, *scratch):
    @pl.when(pl.program_id(0) == 0)
    def _():
        inverse_factor(gram_ref, inverse, *scratch)

    out_ref[...] = exact_dot(inverse[...], basis_ref[0], 1, 0).T * scale


def second_sweep(place, basis, gram, scale):
    count, rank, width = basis.shape
    return pl.pallas_call(
        lambda *refs: second_kernel(scale, *refs),
        out_shape=jax.ShapeDtypeStruct((count * width, rank), f32),
        grid_spec=pltpu.PrefetchScalarGridSpec(
            num_scalar_prefetch=1,
            grid=(count,),
            in_specs=[
                pl.BlockSpec((1, rank, width), lambda i, s: (i, 0, 0)),
                pl.BlockSpec((rank, rank), lambda i, s: (0, 0), pipeline_mode=pl.Buffered(1)),
            ],
            out_specs=pl.BlockSpec((width, rank), lambda i, s: (s[i], 0)),
            scratch_shapes=factor_scratch(rank),
        ),
        name="second_sweep",
    )(place, basis, gram)


def local(interactions, omega):
    user = lax.axis_index("user")
    z, core, x, y = lax.axis_index("item"), user % 2, user // 2 % side, user // (2 * side)
    a = jnp.where(core == 0, x, y)
    b = jnp.where(core == 0, y, x)
    rank = omega.shape[1]
    item_count = omega.shape[0] * lax.axis_size("item")

    far2, high, low = user_rows((z + 2) % side, interactions, omega)
    far2 = shift(far2, "item", 2)
    far1 = shift(user_rows((z + 1) % side, interactions, high, low), "item", 1)
    far3 = shift(user_rows((z + 3) % side, interactions, high, low), "item", 3)
    own = (user_rows(z, interactions, high, low) + far1 + far3 + far2).T
    ys = [shift(own, "item", d) for d in steps]
    place = lambda *d: jnp.stack([*((z - k) % side for k in d), core])

    total = item_columns(place(0), [own], interactions)
    total = item_columns(place(1, 3), ys[:2], interactions, total)
    away = shift(item_columns(place(2), ys[2:], interactions, total, 0), "core")
    kept = item_columns(place(2), ys[2:], interactions, total, 1)

    def scatter(parts, axis, at):
        got = [shift(parts((at + d) % side), axis, d) for d in steps]
        return parts(at) + got[0] + got[1] + got[2]

    at_first = lambda k: lax.dynamic_index_in_dim(kept, k, 0, False) + lax.dynamic_index_in_dim(away, k, 0, False)
    block = scatter(at_first, "first", a)
    block = scatter(lambda k: lax.dynamic_slice_in_dim(block, k * piece, piece, 1), "second", b)
    own_omega = lax.dynamic_slice_in_dim(omega, ((core * side + a) * side + b) * piece, piece, 0)
    block = block + ridge * own_omega.T

    block = jnp.stack([block] + [shift(block, "second", d) for d in steps])
    near = [block] + [shift(block, "first", d) for d in steps]
    far = [shift(part, "core") for part in near]
    slot = jnp.asarray([0, 1, 3, 2])
    slots_at = lambda at: slot[(at - jnp.arange(side)) % side]
    order = jnp.concatenate([slots_at(b), slots_at(a), slots_at(a), slots_at(b), core.reshape(1)]).astype(jnp.int32)
    gram = first_gram(order, near, far)

    def over_items(g):
        h = g.shape[0] // 2
        mine = lax.dynamic_slice_in_dim(g, core * h, h, 0)
        got = [shift(mine, "item", d) for d in steps]
        terms = jnp.stack([mine, *got])
        mine = sum(lax.dynamic_index_in_dim(terms, slot[(z - k) % side], 0, False) for k in range(side))
        other = shift(mine, "core")
        return jnp.concatenate([jnp.where(core == 0, mine, other), jnp.where(core == 0, other, mine)], axis=0)

    basis, gram = first_sweep(order, over_items(gram), [*near, *far])
    offsets = jnp.asarray((0, *steps))
    place = jnp.concatenate([core * side + (a - offsets) % side, (1 - core) * side + (b - offsets) % side])
    return second_sweep(place.astype(jnp.int32), basis, over_items(gram), float(item_count) ** 0.5)


def solution(mesh):
    in_specs = (P("user", "item"), P("item", None))
    out_specs = P("item", None)
    return jax.shard_map(local, mesh=mesh, in_specs=in_specs, out_specs=out_specs, check_vma=False)
```

```python
import jax
import jax.numpy as jnp
from jax import lax
from jax.experimental import pallas as pl
from jax.experimental.pallas import tpu as pltpu
from jax.sharding import PartitionSpec as P

ridge = 200.0
highest = lax.Precision.HIGHEST
f32 = jnp.float32
bf16 = jnp.bfloat16
side = 4
steps = (1, 3, 2)


def exact_dot(a, b, ca, cb):
    return lax.dot_general(a, b, (((ca,), (cb,)), ((), ())), precision=highest, preferred_element_type=f32)


def fast_dot(a, b):
    return lax.dot_general(a, b, (((1,), (0,)), ((), ())), preferred_element_type=f32)


def good_dot(a, b, ca, cb):
    dims = (((ca,), (cb,)), ((), ()))
    dot = lambda l, r: lax.dot_general(l, r, dims, preferred_element_type=f32)
    (a0, a1), (b0, b1) = slices(a), slices(b)
    return dot(a0, b0) + (dot(a0, b1) + dot(a1, b0))


def slices(x):
    high = x.astype(bf16)
    return high, (x - high.astype(f32)).astype(bf16)


def pairs_of(axis, step):
    pairs = []
    for u in range(2 * side * side):
        y, x, core = u // (2 * side), u // 2 % side, u % 2
        if axis == "core":
            core = 1 - core
        elif (axis == "first") == (core == 0):
            x = (x + step) % side
        else:
            y = (y + step) % side
        pairs.append((u, (y * side + x) * 2 + core))
    return pairs


def shift(a, axis, step=1):
    if axis == "item":
        return lax.ppermute(a, "item", [(i, (i + step) % side) for i in range(side)])
    return lax.ppermute(a, "user", pairs_of(axis, step))


vmem = pl.BlockSpec(memory_space=pltpu.VMEM)
smem = pl.BlockSpec(memory_space=pltpu.SMEM)
hbm = pl.BlockSpec(memory_space=pl.ANY)


def rows_kernel(place_ref, a_ref, omega_ref, *refs):
    outs, (high, low) = refs[:-2], refs[-2:]
    at = pl.program_id(0)

    @pl.when(at == 0)
    def _():
        high[...], low[...] = slices(omega_ref[...])

    a = a_ref[...]
    y = (fast_dot(a, high[...]) + fast_dot(a, low[...])).T
    per = pl.num_programs(0) // len(outs)
    for k, out in enumerate(outs):

        @pl.when(at // per == k)
        def _():
            out[...] = y


def user_rows(places, a, omega, block=256):
    users, items = a.shape
    rank = omega.shape[1]
    span = users // side
    per = span // block
    count = len(places)
    return pl.pallas_call(
        rows_kernel,
        out_shape=(jax.ShapeDtypeStruct((rank, span), f32),) * count,
        grid_spec=pltpu.PrefetchScalarGridSpec(
            num_scalar_prefetch=1,
            grid=(per * count,),
            in_specs=[pl.BlockSpec((block, items), lambda i, s: (s[i // per] * per + i % per, 0)), vmem],
            out_specs=tuple(
                pl.BlockSpec((rank, block), lambda i, s, k=k: (0, jnp.clip(i - k * per, 0, per - 1)))
                for k in range(count)
            ),
            scratch_shapes=[pltpu.VMEM((items, rank), bf16)] * 2,
        ),
        name="user_rows",
    )(jnp.stack(places).astype(jnp.int32), a, omega)


def columns_kernel(count, adds, place_ref, *refs):
    ys, blocks = refs[:count], refs[count : 2 * count]
    z_ref, both = refs[-2], refs[-1]
    rank, span = ys[0].shape

    @pl.when(pl.program_id(0) == 0)
    def _():
        for d, ref in enumerate(ys):
            both[:rank, d * span : d * span + span], both[rank:, d * span : d * span + span] = slices(ref[...])

    out = None
    for d, ref in enumerate(blocks):
        term = fast_dot(both[:, d * span : d * span + span], ref[...])
        out = term if out is None else out + term
    z = out[:rank] + out[rank:]
    width = z_ref.shape[2]
    for k in range(z_ref.shape[0]):
        part = z[:, k * width : k * width + width]
        z_ref[k] = part + refs[2 * count][k] if adds else part


def item_columns(place, ys, a, total=None, only=None, block=512):
    users, items = a.shape
    rank, span = ys[0].shape
    count = len(ys)
    width = items // 8
    per = block // width
    grid = items // block // (1 if only is None else 2)
    start = 0 if not only else grid
    in_half = items // block // 2

    def of_items(i, s):
        at = i + start
        core = s[count]
        return (at // in_half + 1 + core) % 2 * in_half + at % in_half

    ins = [pl.BlockSpec((rank, span), lambda i, s: (0, 0), pipeline_mode=pl.Buffered(1))] * count
    for d in range(count):
        ins.append(pl.BlockSpec((span, block), lambda i, s, d=d: (s[d], of_items(i, s))))
    args = [*ys, *[a] * count]
    if total is not None:
        ins.append(pl.BlockSpec((per, rank, width), lambda i, s: (i + start, 0, 0)))
        args.append(total)
    return pl.pallas_call(
        lambda *refs: columns_kernel(count, total is not None, *refs),
        out_shape=jax.ShapeDtypeStruct((grid * per, rank, width), f32),
        grid_spec=pltpu.PrefetchScalarGridSpec(
            num_scalar_prefetch=1,
            grid=(grid,),
            in_specs=ins,
            out_specs=pl.BlockSpec((per, rank, width), lambda i, s: (i, 0, 0)),
            scratch_shapes=[pltpu.VMEM((2 * rank, count * span), bf16)],
        ),
        name="item_columns",
    )(place, *args)


def inverse_factor_half(block):
    n = block.shape[0]
    count = n // 8
    tile = (8, n)
    lanes = lax.broadcasted_iota(jnp.int32, tile, 1)
    subs = lax.broadcasted_iota(jnp.int32, tile, 0)
    spread = lambda v: jnp.broadcast_to(v, tile)
    rows = [block[8 * k : 8 * k + 8, :] for k in range(count)]
    out = []
    for p in range(count):
        c = 8 * p
        panel = rows[p]
        mine = [spread(panel[:, c + t : c + t + 1]) for t in range(8)]
        invs, leads, tops, scale = [], [], [], jnp.ones(tile, f32)
        for j in range(8):
            pivot = spread(mine[j][j : j + 1, :])
            inv = 1.0 / pivot
            invs.append(inv)
            scale = jnp.where(subs == j, pivot, scale)
            factor = jnp.where(subs > j, mine[j] * inv, 0.0)
            tops.append([None] * (j + 1) + [spread(mine[t][j : j + 1, :]) for t in range(j + 1, 8)])
            for t in range(j + 1, 8):
                mine[t] = mine[t] - factor * tops[j][t]
            panel = jnp.where((lanes == c + j) & (subs >= j), jnp.where(subs == j, 1.0, 0.0), panel)
            lead = spread(panel[j : j + 1, :])
            panel = panel - factor * lead
            leads.append(jnp.where((lanes > c + j) & (lanes < c + 8), 0.0, lead))
        out.append(jnp.where(lanes <= subs + c, panel, 0.0) * lax.rsqrt(scale))
        cleared = (lanes >= c) & (lanes < c + 8)
        for k in range(p + 1, count):
            his = [spread(rows[k][:, c + t : c + t + 1]) for t in range(8)]
            new = jnp.where(cleared, 0.0, rows[k])
            for j in range(8):
                factor = his[j] * invs[j]
                for t in range(j + 1, 8):
                    his[t] = his[t] - factor * tops[j][t]
                new = new - factor * leads[j]
            rows[k] = new
    return jnp.concatenate(out, axis=0)


def inverse_factor(gram, out, block, firsts, belows):
    h = block.shape[0]
    block[...] = gram[:h, :h]

    def half(i, carry):
        first = inverse_factor_half(block[...])
        below = exact_dot(gram[h:, :h], first, 1, 1)
        firsts[i] = first
        belows[i] = below
        block[...] = gram[h:, h:] - exact_dot(below, below, 1, 1)
        return carry

    lax.fori_loop(0, 2, half, 0)
    out[:h, :h] = firsts[0]
    out[:h, h:] = jnp.zeros((h, h), f32)
    out[h:, :h] = -exact_dot(firsts[1], exact_dot(belows[0], firsts[0], 1, 0), 1, 0)
    out[h:, h:] = firsts[1]


def factor_scratch(rank):
    h = rank // 2
    return [pltpu.VMEM(shape, f32) for shape in ((rank, rank), (h, h), (2, h, h), (2, h, h))]


def of_ring(own, one, three, two):
    return (own + two) + (one + three)


def mine_of(core_ref, gram):
    h = gram.shape[0] // 2
    return jnp.where(core_ref[0] == 0, gram[:h], gram[h:])


def pair_kernel(near_ref, far_ref, out_ref):
    for k, ref in enumerate((near_ref, far_ref)):
        part = ref[...]
        out_ref[k] = exact_dot(part, part, 1, 1)


def last_pair_kernel(core_ref, near_ref, far_ref, own, one, three, out_ref):
    total = None
    for k, ref in enumerate((near_ref, far_ref)):
        part = ref[...]
        half = of_ring(own[k], one[k], three[k], exact_dot(part, part, 1, 1))
        total = half if total is None else total + half
    out_ref[...] = mine_of(core_ref, total)


def first_gram(core, near, far):
    rank = near[0].shape[0]
    some = [
        pl.pallas_call(
            pair_kernel,
            out_shape=jax.ShapeDtypeStruct((2, rank, rank), f32),
            in_specs=[vmem] * 2,
            out_specs=vmem,
            name="pair_gram",
        )(near[k], far[k])
        for k in range(3)
    ]
    return pl.pallas_call(
        last_pair_kernel,
        out_shape=jax.ShapeDtypeStruct((rank // 2, rank), f32),
        in_specs=[smem] + [vmem] * 5,
        out_specs=vmem,
        name="last_pair_gram",
    )(core, near[3], far[3], *some)


def whole_gram(core_ref, mine_ref, other_ref, gram):
    h = mine_ref.shape[0]
    first = core_ref[0] == 0
    mine, other = mine_ref[...], other_ref[...]
    gram[:h] = jnp.where(first, mine, other)
    gram[h:] = jnp.where(first, other, mine)


def first_kernel(core_ref, mine_ref, other_ref, *refs):
    parts, (basis_ref, out_ref), (held, grams, sems, gram, inverse), scratch = refs[:8], refs[8:10], refs[10:15], refs[15:]
    copies = [pltpu.make_async_copy(ref, held.at[k], sems.at[k]) for k, ref in enumerate(parts)]
    for copy in copies:
        copy.start()
    whole_gram(core_ref, mine_ref, other_ref, gram)
    inverse_factor(gram, inverse, *scratch)
    for copy in copies:
        copy.wait()

    def sweep(k, carry):
        block = exact_dot(inverse[...], held[k], 1, 0)
        basis_ref[k] = block
        grams[k] = good_dot(block, block, 1, 1)
        return carry

    lax.fori_loop(0, 8, sweep, 0)
    halves = [of_ring(*(grams[h * 4 + k] for k in range(4))) for h in range(2)]
    out_ref[...] = mine_of(core_ref, halves[0] + halves[1])


def first_sweep(core, mine, other, parts):
    h, rank = mine.shape
    width = parts[0].shape[1]
    scratch = [pltpu.VMEM((8, rank, width), f32), pltpu.VMEM((8, rank, rank), f32), pltpu.SemaphoreType.DMA((8,))]
    return pl.pallas_call(
        first_kernel,
        out_shape=(jax.ShapeDtypeStruct((8, rank, width), f32), jax.ShapeDtypeStruct((h, rank), f32)),
        in_specs=[smem, vmem, vmem] + [hbm] * 8,
        out_specs=(vmem, vmem),
        scratch_shapes=scratch + [pltpu.VMEM((rank, rank), f32)] + factor_scratch(rank),
        name="first_sweep",
    )(core, mine, other, *parts)


def second_kernel(scale, place_ref, core_ref, mine_ref, other_ref, basis_ref, out_ref, gram, inverse, *scratch):
    @pl.when(pl.program_id(0) == 0)
    def _():
        whole_gram(core_ref, mine_ref, other_ref, gram)
        inverse_factor(gram, inverse, *scratch)

    out_ref[...] = good_dot(inverse[...], basis_ref[0], 1, 0).T * scale


def second_sweep(place, core, mine, other, basis, scale):
    count, rank, width = basis.shape
    return pl.pallas_call(
        lambda *refs: second_kernel(scale, *refs),
        out_shape=jax.ShapeDtypeStruct((count * width, rank), f32),
        grid_spec=pltpu.PrefetchScalarGridSpec(
            num_scalar_prefetch=1,
            grid=(count,),
            in_specs=[smem, vmem, vmem, pl.BlockSpec((1, rank, width), lambda i, s: (i, 0, 0))],
            out_specs=pl.BlockSpec((width, rank), lambda i, s: (s[i], 0)),
            scratch_shapes=[pltpu.VMEM((rank, rank), f32)] + factor_scratch(rank),
        ),
        name="second_sweep",
    )(place, core, mine, other, basis)


def local(interactions, omega):
    user = lax.axis_index("user")
    z, core, x, y = lax.axis_index("item"), user % 2, user // 2 % side, user // (2 * side)
    a = jnp.where(core == 0, x, y)
    b = jnp.where(core == 0, y, x)
    item_count = omega.shape[0] * lax.axis_size("item")
    width = omega.shape[0] // 8
    from_ring = lambda v, axis: [v] + [shift(v, axis, d) for d in steps]

    two, one = user_rows([(z + 2) % side, (z + 1) % side], interactions, omega)
    two, one = shift(two, "item", 2), shift(one, "item", 1)
    three, own = user_rows([(z + 3) % side, z], interactions, omega)
    ys = from_ring(of_ring(own, one, shift(three, "item", 3), two), "item")
    place = lambda *d: jnp.stack([*((z - k) % side for k in d), core])

    total = item_columns(place(0, 1, 3), ys[:3], interactions)
    away = shift(item_columns(place(2), ys[3:], interactions, total, 0), "core")
    kept = item_columns(place(2), ys[3:], interactions, total, 1)

    def block_at(k):
        return lax.dynamic_index_in_dim(kept, k, 0, False) + lax.dynamic_index_in_dim(away, k, 0, False)

    block = of_ring(block_at(a), *(shift(block_at((a + d) % side), "first", d) for d in steps))
    own_omega = lax.dynamic_slice_in_dim(omega, (core * side + a) * width, width, 0)
    block = of_ring(*from_ring(block, "second")) + ridge * own_omega.T

    near = from_ring(block, "first")
    far = [shift(part, "core") for part in near]
    flag = core.reshape(1).astype(jnp.int32)

    def over_items(mine):
        mine = of_ring(*from_ring(mine, "item"))
        return mine, shift(mine, "core")

    basis, gram = first_sweep(flag, *over_items(first_gram(flag, near, far)), [*near, *far])
    offsets = jnp.asarray((0, *steps))
    place = jnp.concatenate([core * side + (a - offsets) % side, (1 - core) * side + (b - offsets) % side])
    return second_sweep(place.astype(jnp.int32), flag, *over_items(gram), basis, float(item_count) ** 0.5)


def solution(mesh):
    in_specs = (P("user", "item"), P("item", None))
    out_specs = P("item", None)
    return jax.shard_map(local, mesh=mesh, in_specs=in_specs, out_specs=out_specs, check_vma=False)
```

```python
import jax
import jax.numpy as jnp
from jax import lax
from jax.experimental import pallas as pl
from jax.experimental.pallas import tpu as pltpu
from jax.sharding import PartitionSpec as P


ridge = 200.0
highest = lax.Precision.HIGHEST
f32 = jnp.float32
bf16 = jnp.bfloat16
side = 4
steps = (1, 3, 2)


def exact_dot(a, b, ca, cb):
    return lax.dot_general(a, b, (((ca,), (cb,)), ((), ())), precision=highest, preferred_element_type=f32)


def fast_dot(a, b):
    return lax.dot_general(a, b, (((1,), (0,)), ((), ())), preferred_element_type=f32)


def good_dot(a, b, ca, cb):
    dims = (((ca,), (cb,)), ((), ()))
    dot = lambda l, r: lax.dot_general(l, r, dims, preferred_element_type=f32)
    (a0, a1), (b0, b1) = slices(a), slices(b)
    return dot(a0, b0) + (dot(a0, b1) + dot(a1, b0))


def slices(x):
    high = x.astype(bf16)
    return high, (x - high.astype(f32)).astype(bf16)


def pairs_of(axis, step):
    pairs = []
    for u in range(2 * side * side):
        y, x, core = u // (2 * side), u // 2 % side, u % 2
        if axis == "core":
            core = 1 - core
        elif (axis == "first") == (core == 0):
            x = (x + step) % side
        else:
            y = (y + step) % side
        pairs.append((u, (y * side + x) * 2 + core))
    return pairs


def shift(a, axis, step=1):
    if axis == "item":
        return lax.ppermute(a, "item", [(i, (i + step) % side) for i in range(side)])
    return lax.ppermute(a, "user", pairs_of(axis, step))


vmem = pl.BlockSpec(memory_space=pltpu.VMEM)
smem = pl.BlockSpec(memory_space=pltpu.SMEM)
hbm = pl.BlockSpec(memory_space=pl.ANY)


def rows_kernel(place_ref, a0, a1, omega_ref, out0, out1, sum0, sum1):
    at, last = pl.program_id(0), pl.num_programs(0) - 1
    high, low = slices(omega_ref[...])
    for ref, total, out in ((a0, sum0, out0), (a1, sum1, out1)):
        a = ref[...]
        y = fast_dot(a, high) + fast_dot(a, low)

        @pl.when(at == 0)
        def _():
            total[...] = y

        @pl.when((at > 0) & (at < last))
        def _():
            total[...] += y

        @pl.when(at == last)
        def _():
            out[...] = (total[...] + y).T


def user_rows(places, a, omega, depth=1024):
    users, items = a.shape
    rank = omega.shape[1]
    span = users // side
    out = pl.BlockSpec((rank, span), lambda k, s: (0, 0))
    return pl.pallas_call(
        rows_kernel,
        out_shape=(jax.ShapeDtypeStruct((rank, span), f32),) * 2,
        grid_spec=pltpu.PrefetchScalarGridSpec(
            num_scalar_prefetch=1,
            grid=(items // depth,),
            in_specs=[pl.BlockSpec((span, depth), lambda k, s, d=d: (s[d], k)) for d in range(2)]
            + [pl.BlockSpec((depth, rank), lambda k, s: (k, 0))],
            out_specs=(out, out),
            scratch_shapes=[pltpu.VMEM((span, rank), f32)] * 2,
        ),
        name="user_rows",
    )(jnp.stack(places).astype(jnp.int32), a, a, omega)


def columns_kernel(count, splits, adds, place_ref, *refs):
    ys, blocks = refs[: count * splits], refs[count * splits : count * splits + count]
    z_ref, both = refs[-2], refs[-1]
    rows, span = ys[0].shape
    rank = rows * splits

    @pl.when(pl.program_id(0) == 0)
    def _():
        for d, ref in enumerate(ys):
            at = slice(d // splits * span, d // splits * span + span)
            row = d % splits * rows
            both[row : row + rows, at], both[rank + row : rank + row + rows, at] = slices(ref[...])

    out = None
    for d, ref in enumerate(blocks):
        term = fast_dot(both[:, d * span : d * span + span], ref[...])
        out = term if out is None else out + term
    z = out[:rank] + out[rank:]
    width = z_ref.shape[2]
    for k in range(z_ref.shape[0]):
        part = z[:, k * width : k * width + width]
        z_ref[k] = part + refs[-3][k] if adds else part


def item_columns(place, ys, a, total=None, only=None, splits=1, block=1024):
    _, items = a.shape
    rows, span = ys[0].shape
    rank = rows * splits
    count = len(ys) // splits
    width = items // 8
    per = block // width
    grid = items // block // (1 if only is None else 2)
    start = 0 if not only else grid
    in_half = items // block // 2

    def of_items(i, s):
        at = i + start
        core = s[count]
        return (at // in_half + 1 + core) % 2 * in_half + at % in_half

    ins = [vmem] * len(ys)
    for d in range(count):
        ins.append(pl.BlockSpec((span, block), lambda i, s, d=d: (s[d], of_items(i, s))))
    args = [*ys, *[a] * count]
    if total is not None:
        ins.append(pl.BlockSpec((per, rank, width), lambda i, s: (i + start, 0, 0)))
        args.append(total)
    return pl.pallas_call(
        lambda *refs: columns_kernel(count, splits, total is not None, *refs),
        out_shape=jax.ShapeDtypeStruct((grid * per, rank, width), f32),
        grid_spec=pltpu.PrefetchScalarGridSpec(
            num_scalar_prefetch=1,
            grid=(grid,),
            in_specs=ins,
            out_specs=pl.BlockSpec((per, rank, width), lambda i, s: (i, 0, 0)),
            scratch_shapes=[pltpu.VMEM((2 * rank, count * span), bf16)],
        ),
        name="item_columns",
    )(place, *args)


def inverse_factor_half(block):
    n = block.shape[0]
    count = n // 8
    tile = (8, n)
    lanes = lax.broadcasted_iota(jnp.int32, tile, 1)
    subs = lax.broadcasted_iota(jnp.int32, tile, 0)
    spread = lambda v: jnp.broadcast_to(v, tile)
    rows = [block[8 * k : 8 * k + 8, :] for k in range(count)]
    out = []
    for p in range(count):
        c = 8 * p
        panel = rows[p]
        mine = [spread(panel[:, c + t : c + t + 1]) for t in range(8)]
        invs, leads, tops, scale = [], [], [], jnp.ones(tile, f32)
        for j in range(8):
            pivot = spread(mine[j][j : j + 1, :])
            inv = 1.0 / pivot
            invs.append(inv)
            scale = jnp.where(subs == j, pivot, scale)
            factor = jnp.where(subs > j, mine[j] * inv, 0.0)
            tops.append([None] * (j + 1) + [spread(mine[t][j : j + 1, :]) for t in range(j + 1, 8)])
            for t in range(j + 1, 8):
                mine[t] = mine[t] - factor * tops[j][t]
            panel = jnp.where((lanes == c + j) & (subs >= j), jnp.where(subs == j, 1.0, 0.0), panel)
            lead = spread(panel[j : j + 1, :])
            panel = panel - factor * lead
            leads.append(jnp.where((lanes > c + j) & (lanes < c + 8), 0.0, lead))
        out.append(jnp.where(lanes <= subs + c, panel, 0.0) * lax.rsqrt(scale))
        cleared = (lanes >= c) & (lanes < c + 8)
        for k in range(p + 1, count):
            his = [spread(rows[k][:, c + t : c + t + 1]) for t in range(8)]
            new = jnp.where(cleared, 0.0, rows[k])
            for j in range(8):
                factor = his[j] * invs[j]
                for t in range(j + 1, 8):
                    his[t] = his[t] - factor * tops[j][t]
                new = new - factor * leads[j]
            rows[k] = new
    return jnp.concatenate(out, axis=0)


def inverse_factor(gram, out, block, firsts, belows):
    h = block.shape[0]
    block[...] = gram[:h, :h]

    def half(i, carry):
        first = inverse_factor_half(block[...])
        below = exact_dot(gram[h:, :h], first, 1, 1)
        firsts[i] = first
        belows[i] = below
        block[...] = gram[h:, h:] - exact_dot(below, below, 1, 1)
        return carry

    lax.fori_loop(0, 2, half, 0)
    out[:h, :h] = firsts[0]
    out[:h, h:] = jnp.zeros((h, h), f32)
    out[h:, :h] = -exact_dot(firsts[1], exact_dot(belows[0], firsts[0], 1, 0), 1, 0)
    out[h:, h:] = firsts[1]


def inverse_factor_near_one(gram, out):
    n = gram.shape[0]
    row = lax.broadcasted_iota(jnp.int32, (n, n), 0)
    column = lax.broadcasted_iota(jnp.int32, (n, n), 1)
    one = jnp.where(row == column, 1.0, 0.0)
    lower = jnp.where(row > column, 1.0, jnp.where(row == column, 0.5, 0.0))
    out[...] = one - lower * (gram[...] - one)

    def more(state):
        return (state[1] > 1e-7) & (state[0] < 6)

    def step(state):
        inverse = out[...]
        residual = exact_dot(exact_dot(inverse, gram[...], 1, 0), inverse, 1, 1) - one
        out[...] = inverse - exact_dot(lower * residual, inverse, 1, 0)
        return state[0] + 1, jnp.sum(residual * residual)

    return lax.while_loop(more, step, (0, jnp.float32(1.0)))[1] <= 1e-7


def factor_scratch(rank):
    h = rank // 2
    return [pltpu.VMEM(shape, f32) for shape in ((rank, rank), (h, h), (2, h, h), (2, h, h))]


def of_ring(own, one, three, two):
    return (own + two) + (one + three)


def mine_of(core_ref, gram):
    h, q = gram.shape[0] // 2, gram.shape[0] // 4
    one = jnp.concatenate([gram[:h, :h], gram[h : h + q, :h]], axis=0)
    two = jnp.concatenate([gram[h:, h:], gram[h + q :, :h]], axis=0)
    return jnp.where(core_ref[0] == 0, one, two)


def packed(rank):
    return jax.ShapeDtypeStruct((rank // 2 + rank // 4, rank // 2), f32)


def pair_kernel(near_ref, far_ref, out_ref):
    for k, ref in enumerate((near_ref, far_ref)):
        part = ref[...]
        out_ref[k] = exact_dot(part, part, 1, 1)


def last_pairs_kernel(core_ref, own_ref, *refs):
    near, far, out_ref = refs[:3], refs[3:6], refs[6]
    total = None
    for k, parts in enumerate((near, far)):
        grams = [exact_dot(ref[...], ref[...], 1, 1) for ref in parts]
        half = of_ring(own_ref[k], *grams)
        total = half if total is None else total + half
    out_ref[...] = mine_of(core_ref, total)


def first_gram(core, near, far):
    rank = near[0].shape[0]
    own = pl.pallas_call(
        pair_kernel,
        out_shape=jax.ShapeDtypeStruct((2, rank, rank), f32),
        in_specs=[vmem] * 2,
        out_specs=vmem,
        name="pair_gram",
    )(near[0], far[0])
    return pl.pallas_call(
        last_pairs_kernel,
        out_shape=packed(rank),
        in_specs=[smem] + [vmem] * 7,
        out_specs=vmem,
        name="last_pair_grams",
    )(core, own, *near[1:], *far[1:])


def whole_gram(core_ref, mine_ref, other_ref, gram):
    h = gram.shape[0] // 2
    mine, other = mine_ref[...], other_ref[...]
    one = jnp.where(core_ref[0] == 0, mine, other)
    two = jnp.where(core_ref[0] == 0, other, mine)
    below = jnp.concatenate([one[h:], two[h:]], axis=0)
    gram[:h, :h], gram[:h, h:] = one[:h], below.T
    gram[h:, :h], gram[h:, h:] = below, two[:h]


def first_kernel(core_ref, mine_ref, other_ref, *refs):
    parts, (basis_ref, out_ref), (held, grams, sems, gram, inverse), scratch = refs[:8], refs[8:10], refs[10:15], refs[15:]
    copies = [pltpu.make_async_copy(ref, held.at[k], sems.at[k]) for k, ref in enumerate(parts)]
    for copy in copies:
        copy.start()
    whole_gram(core_ref, mine_ref, other_ref, gram)
    inverse_factor(gram, inverse, *scratch)
    for copy in copies:
        copy.wait()

    def sweep(k, carry):
        block = exact_dot(inverse[...], held[k], 1, 0)
        basis_ref[k] = block
        grams[k] = good_dot(block, block, 1, 1)
        return carry

    lax.fori_loop(0, 8, sweep, 0, unroll=2)
    halves = [of_ring(*(grams[h * 4 + k] for k in range(4))) for h in range(2)]
    out_ref[...] = mine_of(core_ref, halves[0] + halves[1])


def first_sweep(core, mine, other, parts):
    rank, width = parts[0].shape
    scratch = [pltpu.VMEM((8, rank, width), f32), pltpu.VMEM((8, rank, rank), f32), pltpu.SemaphoreType.DMA((8,))]
    return pl.pallas_call(
        first_kernel,
        out_shape=(jax.ShapeDtypeStruct((8, rank, width), f32), packed(rank)),
        in_specs=[smem, vmem, vmem] + [hbm] * 8,
        out_specs=(vmem, vmem),
        scratch_shapes=scratch + [pltpu.VMEM((rank, rank), f32)] + factor_scratch(rank),
        name="first_sweep",
    )(core, mine, other, *parts)


def second_kernel(scale, place_ref, core_ref, mine_ref, other_ref, basis_ref, out_ref, gram, inverse, *scratch):
    @pl.when(pl.program_id(0) == 0)
    def _():
        whole_gram(core_ref, mine_ref, other_ref, gram)
        converged = inverse_factor_near_one(gram, inverse)

        @pl.when(jnp.logical_not(converged))
        def _():
            inverse_factor(gram, inverse, *scratch)

    out_ref[...] = good_dot(inverse[...], basis_ref[0], 1, 0).T * scale


def second_sweep(place, core, mine, other, basis, scale):
    count, rank, width = basis.shape
    return pl.pallas_call(
        lambda *refs: second_kernel(scale, *refs),
        out_shape=jax.ShapeDtypeStruct((count * width, rank), f32),
        grid_spec=pltpu.PrefetchScalarGridSpec(
            num_scalar_prefetch=1,
            grid=(count,),
            in_specs=[smem, vmem, vmem, pl.BlockSpec((1, rank, width), lambda i, s: (i, 0, 0))],
            out_specs=pl.BlockSpec((width, rank), lambda i, s: (s[i], 0)),
            scratch_shapes=[pltpu.VMEM((rank, rank), f32)] + factor_scratch(rank),
        ),
        name="second_sweep",
    )(place, core, mine, other, basis)


def program(interactions, omega):
    user = lax.axis_index("user")
    z, core, x, y = lax.axis_index("item"), user % 2, user // 2 % side, user // (2 * side)
    a = jnp.where(core == 0, x, y)
    b = jnp.where(core == 0, y, x)
    item_count = omega.shape[0] * lax.axis_size("item")
    width = omega.shape[0] // 8
    from_ring = lambda v, axis: [v] + [shift(v, axis, d) for d in steps]

    two, one = user_rows([(z + 2) % side, (z + 1) % side], interactions, omega)
    two, one = shift(two, "item", 2), shift(one, "item", 1)
    three, own = user_rows([(z + 3) % side, z], interactions, omega)
    own = of_ring(own, one, shift(three, "item", 3), two)
    one, three = shift(own, "item", 1), shift(own, "item", 3)
    half = own.shape[0] // 2
    two = [shift(one[:half], "item", 1), shift(three[half:], "item", 3)]
    place = lambda *d: jnp.stack([*((z - k) % side for k in d), core])

    total = item_columns(place(0, 1, 3), [own, one, three], interactions)
    away = shift(item_columns(place(2), two, interactions, total, 0, 2), "core")
    kept = item_columns(place(2), two, interactions, total, 1, 2)

    def block_at(k):
        return lax.dynamic_index_in_dim(kept, k, 0, False) + lax.dynamic_index_in_dim(away, k, 0, False)

    block = of_ring(block_at(a), *(shift(block_at((a + d) % side), "first", d) for d in steps))
    own_omega = lax.dynamic_slice_in_dim(omega, (core * side + a) * width, width, 0)
    block = of_ring(*from_ring(block, "second")) + ridge * own_omega.T

    near = from_ring(block, "first")
    far = [shift(part, "core") for part in near]
    flag = core.reshape(1).astype(jnp.int32)

    def over_items(mine):
        mine = of_ring(*from_ring(mine, "item"))
        return mine, shift(mine, "core")

    basis, gram = first_sweep(flag, *over_items(first_gram(flag, near, far)), [*near, *far])
    offsets = jnp.asarray((0, *steps))
    place = jnp.concatenate([core * side + (a - offsets) % side, (1 - core) * side + (b - offsets) % side])
    return second_sweep(place.astype(jnp.int32), flag, *over_items(gram), basis, float(item_count) ** 0.5)


def solution(mesh):
    in_specs = (P("user", "item"), P("item", None))
    out_specs = P("item", None)
    return jax.shard_map(program, mesh=mesh, in_specs=in_specs, out_specs=out_specs, check_vma=False)
```

```python
import jax
import jax.numpy as jnp
from jax import lax
from jax.experimental import pallas as pl
from jax.experimental.pallas import tpu as pltpu
from jax.sharding import PartitionSpec as P


ridge = 200.0
highest = lax.Precision.HIGHEST
f32 = jnp.float32
bf16 = jnp.bfloat16
side = 4
steps = (1, 3, 2)


def exact_dot(a, b, ca, cb):
    return lax.dot_general(a, b, (((ca,), (cb,)), ((), ())), precision=highest, preferred_element_type=f32)


def fast_dot(a, b):
    return lax.dot_general(a, b, (((1,), (0,)), ((), ())), preferred_element_type=f32)


def good_dot(a, b, ca, cb):
    dims = (((ca,), (cb,)), ((), ()))
    dot = lambda l, r: lax.dot_general(l, r, dims, preferred_element_type=f32)
    (a0, a1), (b0, b1) = slices(a), slices(b)
    return dot(a0, b0) + (dot(a0, b1) + dot(a1, b0))


def slices(x):
    high = x.astype(bf16)
    return high, (x - high.astype(f32)).astype(bf16)


def pairs_of(axis, step):
    pairs = []
    for u in range(2 * side * side):
        y, x, core = u // (2 * side), u // 2 % side, u % 2
        if axis == "core":
            core = 1 - core
        elif (axis == "first") == (core == 0):
            x = (x + step) % side
        else:
            y = (y + step) % side
        pairs.append((u, (y * side + x) * 2 + core))
    return pairs


def shift(a, axis, step=1):
    if axis == "item":
        return lax.ppermute(a, "item", [(i, (i + step) % side) for i in range(side)])
    return lax.ppermute(a, "user", pairs_of(axis, step))


vmem = pl.BlockSpec(memory_space=pltpu.VMEM)
smem = pl.BlockSpec(memory_space=pltpu.SMEM)
hbm = pl.BlockSpec(memory_space=pl.ANY)


def rows_kernel(place_ref, a0, a1, omega_ref, out0, out1, total):
    at, last = pl.program_id(0), pl.num_programs(0) - 1
    span = a0.shape[0]
    high, low = slices(omega_ref[...])
    a = jnp.concatenate([a0[...], a1[...]], axis=0)
    y = fast_dot(a, high) + fast_dot(a, low)

    @pl.when(at == 0)
    def _():
        total[...] = y

    @pl.when((at > 0) & (at < last))
    def _():
        total[...] += y

    @pl.when(at == last)
    def _():
        whole = total[...] + y
        out0[...], out1[...] = whole[:span].T, whole[span:].T


def user_rows(place, at, a, omega, depth=1024):
    users, items = a.shape
    rank = omega.shape[1]
    span = users // side
    out = pl.BlockSpec((rank, span), lambda k, s: (0, 0))
    return pl.pallas_call(
        rows_kernel,
        out_shape=(jax.ShapeDtypeStruct((rank, span), f32),) * 2,
        grid_spec=pltpu.PrefetchScalarGridSpec(
            num_scalar_prefetch=1,
            grid=(items // depth,),
            in_specs=[pl.BlockSpec((span, depth), lambda k, s, d=d: (s[at + d], k)) for d in range(2)]
            + [pl.BlockSpec((depth, rank), lambda k, s: (k, 0))],
            out_specs=(out, out),
            scratch_shapes=[pltpu.VMEM((2 * span, rank), f32)],
        ),
        name="user_rows",
    )(place, a, a, omega)


def columns_kernel(count, splits, adds, place_ref, *refs):
    ys, blocks = refs[: count * splits], refs[count * splits : count * splits + count]
    z_ref, both = refs[-2], refs[-1]
    rows, span = ys[0].shape
    rank = rows * splits

    @pl.when(pl.program_id(0) == 0)
    def _():
        for d, ref in enumerate(ys):
            at = slice(d // splits * span, d // splits * span + span)
            row = d % splits * rows
            both[row : row + rows, at], both[rank + row : rank + row + rows, at] = slices(ref[...])

    out = None
    for d, ref in enumerate(blocks):
        term = fast_dot(both[:, d * span : d * span + span], ref[...])
        out = term if out is None else out + term
    z = out[:rank] + out[rank:]
    width = z_ref.shape[2]
    for k in range(z_ref.shape[0]):
        part = z[:, k * width : k * width + width]
        z_ref[k] = part + refs[-3][k] if adds else part


def item_columns(place, start_at, ys, a, total=None, only=None, splits=1, block=1024):
    _, items = a.shape
    rows, span = ys[0].shape
    rank = rows * splits
    count = len(ys) // splits
    width = items // 8
    per = block // width
    grid = items // block // (1 if only is None else 2)
    start = 0 if not only else grid
    in_half = items // block // 2

    def of_items(i, s):
        at = i + start
        core = s[place.shape[0] - 1]
        return (at // in_half + 1 + core) % 2 * in_half + at % in_half

    ins = [pl.BlockSpec((rows, span), lambda i, s: (0, 0), pipeline_mode=pl.Buffered(1))] * len(ys)
    for d in range(count):
        ins.append(pl.BlockSpec((span, block), lambda i, s, d=d: (s[start_at + d], of_items(i, s))))
    args = [*ys, *[a] * count]
    if total is not None:
        ins.append(pl.BlockSpec((per, rank, width), lambda i, s: (i + start, 0, 0)))
        args.append(total)
    return pl.pallas_call(
        lambda *refs: columns_kernel(count, splits, total is not None, *refs),
        out_shape=jax.ShapeDtypeStruct((grid * per, rank, width), f32),
        grid_spec=pltpu.PrefetchScalarGridSpec(
            num_scalar_prefetch=1,
            grid=(grid,),
            in_specs=ins,
            out_specs=pl.BlockSpec((per, rank, width), lambda i, s: (i, 0, 0)),
            scratch_shapes=[pltpu.VMEM((2 * rank, count * span), bf16)],
        ),
        name="item_columns",
    )(place, *args)


def inverse_factor_half(block):
    n = block.shape[0]
    count = n // 8
    tile = (8, n)
    lanes = lax.broadcasted_iota(jnp.int32, tile, 1)
    subs = lax.broadcasted_iota(jnp.int32, tile, 0)
    spread = lambda v: jnp.broadcast_to(v, tile)
    rows = [block[8 * k : 8 * k + 8, :] for k in range(count)]
    out = []
    for p in range(count):
        c = 8 * p
        panel = rows[p]
        mine = [spread(panel[:, c + t : c + t + 1]) for t in range(8)]
        invs, leads, tops, scale = [], [], [], jnp.ones(tile, f32)
        for j in range(8):
            pivot = spread(mine[j][j : j + 1, :])
            inv = 1.0 / pivot
            invs.append(inv)
            scale = jnp.where(subs == j, pivot, scale)
            factor = jnp.where(subs > j, mine[j] * inv, 0.0)
            tops.append([None] * (j + 1) + [spread(mine[t][j : j + 1, :]) for t in range(j + 1, 8)])
            for t in range(j + 1, 8):
                mine[t] = mine[t] - factor * tops[j][t]
            panel = jnp.where((lanes == c + j) & (subs >= j), jnp.where(subs == j, 1.0, 0.0), panel)
            lead = spread(panel[j : j + 1, :])
            panel = panel - factor * lead
            leads.append(jnp.where((lanes > c + j) & (lanes < c + 8), 0.0, lead))
        out.append(jnp.where(lanes <= subs + c, panel, 0.0) * lax.rsqrt(scale))
        cleared = (lanes >= c) & (lanes < c + 8)
        for k in range(p + 1, count):
            his = [spread(rows[k][:, c + t : c + t + 1]) for t in range(8)]
            new = jnp.where(cleared, 0.0, rows[k])
            for j in range(8):
                factor = his[j] * invs[j]
                for t in range(j + 1, 8):
                    his[t] = his[t] - factor * tops[j][t]
                new = new - factor * leads[j]
            rows[k] = new
    return jnp.concatenate(out, axis=0)


def inverse_factor(gram, out, block, firsts, belows):
    h = block.shape[0]
    block[...] = gram[:h, :h]

    def half(i, carry):
        first = inverse_factor_half(block[...])
        below = exact_dot(gram[h:, :h], first, 1, 1)
        firsts[i] = first
        belows[i] = below
        block[...] = gram[h:, h:] - exact_dot(below, below, 1, 1)
        return carry

    lax.fori_loop(0, 2, half, 0)
    out[:h, :h] = firsts[0]
    out[:h, h:] = jnp.zeros((h, h), f32)
    out[h:, :h] = -exact_dot(firsts[1], exact_dot(belows[0], firsts[0], 1, 0), 1, 0)
    out[h:, h:] = firsts[1]


def inverse_factor_near_one(gram, out):
    n = gram.shape[0]
    row = lax.broadcasted_iota(jnp.int32, (n, n), 0)
    column = lax.broadcasted_iota(jnp.int32, (n, n), 1)
    one = jnp.where(row == column, 1.0, 0.0)
    lower = jnp.where(row > column, 1.0, jnp.where(row == column, 0.5, 0.0))
    out[...] = one - lower * (gram[...] - one)

    def more(state):
        return (state[1] > 1e-7) & (state[0] < 6)

    def step(state):
        inverse = out[...]
        residual = exact_dot(exact_dot(inverse, gram[...], 1, 0), inverse, 1, 1) - one
        out[...] = inverse - exact_dot(lower * residual, inverse, 1, 0)
        return state[0] + 1, jnp.sum(residual * residual)

    return lax.while_loop(more, step, (0, jnp.float32(1.0)))[1] <= 1e-7


def factor_scratch(rank):
    h = rank // 2
    return [pltpu.VMEM(shape, f32) for shape in ((rank, rank), (h, h), (2, h, h), (2, h, h))]


def of_ring(own, one, three, two):
    return (own + two) + (one + three)


def mine_of(core_ref, gram):
    h, q = gram.shape[0] // 2, gram.shape[0] // 4
    one = jnp.concatenate([gram[:h, :h], gram[h : h + q, :h]], axis=0)
    two = jnp.concatenate([gram[h:, h:], gram[h + q :, :h]], axis=0)
    return jnp.where(core_ref[0] == 0, one, two)


def packed(rank):
    return jax.ShapeDtypeStruct((rank // 2 + rank // 4, rank // 2), f32)


def pair_kernel(near_ref, far_ref, out_ref):
    for k, ref in enumerate((near_ref, far_ref)):
        part = ref[...]
        out_ref[k] = exact_dot(part, part, 1, 1)


def last_pairs_kernel(core_ref, own_ref, *refs):
    near, far, out_ref = refs[:3], refs[3:6], refs[6]
    total = None
    for k, parts in enumerate((near, far)):
        grams = [exact_dot(ref[...], ref[...], 1, 1) for ref in parts]
        half = of_ring(own_ref[k], *grams)
        total = half if total is None else total + half
    out_ref[...] = mine_of(core_ref, total)


def first_gram(core, near, far):
    rank = near[0].shape[0]
    own = pl.pallas_call(
        pair_kernel,
        out_shape=jax.ShapeDtypeStruct((2, rank, rank), f32),
        in_specs=[vmem] * 2,
        out_specs=vmem,
        name="pair_gram",
    )(near[0], far[0])
    return pl.pallas_call(
        last_pairs_kernel,
        out_shape=packed(rank),
        in_specs=[smem] + [vmem] * 7,
        out_specs=vmem,
        name="last_pair_grams",
    )(core, own, *near[1:], *far[1:])


def whole_gram(core_ref, mine_ref, other_ref, gram):
    h = gram.shape[0] // 2
    mine, other = mine_ref[...], other_ref[...]
    one = jnp.where(core_ref[0] == 0, mine, other)
    two = jnp.where(core_ref[0] == 0, other, mine)
    below = jnp.concatenate([one[h:], two[h:]], axis=0)
    gram[:h, :h], gram[:h, h:] = one[:h], below.T
    gram[h:, :h], gram[h:, h:] = below, two[:h]


def first_kernel(core_ref, slot_ref, mine_ref, other_ref, *refs):
    parts, (basis_ref, out_ref), (held, grams, sems, gram, inverse), scratch = refs[:8], refs[8:10], refs[10:15], refs[15:]
    copies = [pltpu.make_async_copy(ref, held.at[k], sems.at[k]) for k, ref in enumerate(parts)]
    for copy in copies:
        copy.start()
    whole_gram(core_ref, mine_ref, other_ref, gram)
    inverse_factor(gram, inverse, *scratch)
    for copy in copies:
        copy.wait()

    def sweep(k, carry):
        block = exact_dot(inverse[...], held[k], 1, 0)
        basis_ref[slot_ref[k]] = block
        grams[k] = good_dot(block, block, 1, 1)
        return carry

    lax.fori_loop(0, 8, sweep, 0, unroll=4)
    halves = [of_ring(*(grams[h * 4 + k] for k in range(4))) for h in range(2)]
    out_ref[...] = mine_of(core_ref, halves[0] + halves[1])


def first_sweep(core, slots, mine, other, parts):
    rank, width = parts[0].shape
    scratch = [pltpu.VMEM((8, rank, width), f32), pltpu.VMEM((8, rank, rank), f32), pltpu.SemaphoreType.DMA((8,))]
    return pl.pallas_call(
        first_kernel,
        out_shape=(jax.ShapeDtypeStruct((8, rank, width), f32), packed(rank)),
        in_specs=[smem, smem, vmem, vmem] + [hbm] * 8,
        out_specs=(vmem, vmem),
        scratch_shapes=scratch + [pltpu.VMEM((rank, rank), f32)] + factor_scratch(rank),
        name="first_sweep",
    )(core, slots, mine, other, *parts)


def second_kernel(scale, core_ref, mine_ref, other_ref, basis_ref, out_ref, gram, inverse, *scratch):
    @pl.when(pl.program_id(0) == 0)
    def _():
        whole_gram(core_ref, mine_ref, other_ref, gram)
        converged = inverse_factor_near_one(gram, inverse)

        @pl.when(jnp.logical_not(converged))
        def _():
            inverse_factor(gram, inverse, *scratch)

    width = basis_ref.shape[2]
    for k in range(basis_ref.shape[0]):
        out_ref[k * width : k * width + width] = good_dot(basis_ref[k], inverse[...], 0, 1) * scale


def second_sweep(core, mine, other, basis, scale, per=2):
    count, rank, width = basis.shape
    return pl.pallas_call(
        lambda *refs: second_kernel(scale, *refs),
        out_shape=jax.ShapeDtypeStruct((count * width, rank), f32),
        grid=(count // per,),
        in_specs=[smem, vmem, vmem, pl.BlockSpec((per, rank, width), lambda i: (i, 0, 0))],
        out_specs=pl.BlockSpec((per * width, rank), lambda i: (i, 0)),
        scratch_shapes=[pltpu.VMEM((rank, rank), f32)] + factor_scratch(rank),
        name="second_sweep",
    )(core, mine, other, basis)


def program(interactions, omega):
    user = lax.axis_index("user")
    z, core, x, y = lax.axis_index("item"), user % 2, user // 2 % side, user // (2 * side)
    a = jnp.where(core == 0, x, y)
    b = jnp.where(core == 0, y, x)
    item_count = omega.shape[0] * lax.axis_size("item")
    width = omega.shape[0] // 8
    from_ring = lambda v, axis: [v] + [shift(v, axis, d) for d in steps]

    place = jnp.stack([*((z + k) % side for k in (2, 1, 3, 0, 3, 1, 2)), core]).astype(jnp.int32)
    offsets = jnp.asarray((0, *steps))
    slots = jnp.concatenate([core * side + (a - offsets) % side, (1 - core) * side + (b - offsets) % side])

    two, one = user_rows(place, 0, interactions, omega)
    two, one = shift(two, "item", 2), shift(one, "item", 1)
    three, own = user_rows(place, 2, interactions, omega)
    own = of_ring(own, one, shift(three, "item", 3), two)
    one, three = shift(own, "item", 1), shift(own, "item", 3)
    half = own.shape[0] // 2
    two = [shift(one[:half], "item", 1), shift(three[half:], "item", 3)]

    total = item_columns(place, 3, [own], interactions)
    total = item_columns(place, 4, [one, three], interactions, total)
    away = shift(item_columns(place, 6, two, interactions, total, 0, 2), "core")
    kept = item_columns(place, 6, two, interactions, total, 1, 2)

    def block_at(k):
        return lax.dynamic_index_in_dim(kept, k, 0, False) + lax.dynamic_index_in_dim(away, k, 0, False)

    block = of_ring(block_at(a), *(shift(block_at((a + d) % side), "first", d) for d in steps))
    own_omega = lax.dynamic_slice_in_dim(omega, (core * side + a) * width, width, 0)
    block = of_ring(*from_ring(block, "second")) + ridge * own_omega.T

    near = from_ring(block, "first")
    far = [shift(part, "core") for part in near]
    flag = core.reshape(1).astype(jnp.int32)

    def over_items(mine):
        mine = of_ring(*from_ring(mine, "item"))
        return mine, shift(mine, "core")

    basis, gram = first_sweep(flag, slots.astype(jnp.int32), *over_items(first_gram(flag, near, far)), [*near, *far])
    return second_sweep(flag, *over_items(gram), basis, float(item_count) ** 0.5)


def solution(mesh):
    in_specs = (P("user", "item"), P("item", None))
    out_specs = P("item", None)
    return jax.shard_map(program, mesh=mesh, in_specs=in_specs, out_specs=out_specs, check_vma=False)
```

```python
import jax
import jax.numpy as jnp
from jax import lax
from jax.experimental import pallas as pl
from jax.experimental.pallas import tpu as pltpu
from jax.sharding import PartitionSpec as P


ridge = 200.0
highest = lax.Precision.HIGHEST
f32 = jnp.float32
bf16 = jnp.bfloat16
side = 4
steps = (1, 3, 2)


def exact_dot(a, b, ca, cb):
    return lax.dot_general(a, b, (((ca,), (cb,)), ((), ())), precision=highest, preferred_element_type=f32)


def fast_dot(a, b):
    return lax.dot_general(a, b, (((1,), (0,)), ((), ())), preferred_element_type=f32)


def good_dot(a, b, ca, cb):
    dims = (((ca,), (cb,)), ((), ()))
    dot = lambda l, r: lax.dot_general(l, r, dims, preferred_element_type=f32)
    (a0, a1), (b0, b1) = slices(a), slices(b)
    return dot(a0, b0) + (dot(a0, b1) + dot(a1, b0))


def slices(x):
    high = x.astype(bf16)
    return high, (x - high.astype(f32)).astype(bf16)


def pairs_of(axis, step):
    pairs = []
    for u in range(2 * side * side):
        y, x, core = u // (2 * side), u // 2 % side, u % 2
        if axis == "core":
            core = 1 - core
        elif (axis == "first") == (core == 0):
            x = (x + step) % side
        else:
            y = (y + step) % side
        pairs.append((u, (y * side + x) * 2 + core))
    return pairs


def shift(a, axis, step=1):
    if axis == "item":
        return lax.ppermute(a, "item", [(i, (i + step) % side) for i in range(side)])
    return lax.ppermute(a, "user", pairs_of(axis, step))


vmem = pl.BlockSpec(memory_space=pltpu.VMEM)
smem = pl.BlockSpec(memory_space=pltpu.SMEM)
hbm = pl.BlockSpec(memory_space=pl.ANY)


def rows_kernel(count, place_ref, *refs):
    quarters, omega_ref, outs, total = refs[:count], refs[count], refs[count + 1 : -1], refs[-1]
    at, last = pl.program_id(0), pl.num_programs(0) - 1
    span = quarters[0].shape[0]
    high, low = slices(omega_ref[...])
    a = jnp.concatenate([ref[...] for ref in quarters], axis=0)
    y = fast_dot(a, high) + fast_dot(a, low)

    @pl.when(at == 0)
    def _():
        total[...] = y

    @pl.when((at > 0) & (at < last))
    def _():
        total[...] += y

    @pl.when(at == last)
    def _():
        whole = total[...] + y
        for d, out in enumerate(outs):
            out[...] = whole[d * span : d * span + span].T


def user_rows(place, at, count, a, omega, depth=1024):
    users, items = a.shape
    rank = omega.shape[1]
    span = users // side
    return pl.pallas_call(
        lambda *refs: rows_kernel(count, *refs),
        out_shape=(jax.ShapeDtypeStruct((rank, span), f32),) * count,
        grid_spec=pltpu.PrefetchScalarGridSpec(
            num_scalar_prefetch=1,
            grid=(items // depth,),
            in_specs=[pl.BlockSpec((span, depth), lambda k, s, d=d: (s[at + d], k)) for d in range(count)]
            + [pl.BlockSpec((depth, rank), lambda k, s: (k, 0))],
            out_specs=(pl.BlockSpec((rank, span), lambda k, s: (0, 0)),) * count,
            scratch_shapes=[pltpu.VMEM((count * span, rank), f32)],
        ),
        name="user_rows",
    )(place, *[a] * count, omega)


def columns_kernel(count, splits, adds, place_ref, *refs):
    ys, blocks = refs[: count * splits], refs[count * splits : count * splits + count]
    z_ref, both = refs[-2], refs[-1]
    rows, span = ys[0].shape
    rank = rows * splits

    @pl.when(pl.program_id(0) == 0)
    def _():
        for d, ref in enumerate(ys):
            at = slice(d // splits * span, d // splits * span + span)
            row = d % splits * rows
            both[row : row + rows, at], both[rank + row : rank + row + rows, at] = slices(ref[...])

    out = None
    for d, ref in enumerate(blocks):
        term = fast_dot(both[:, d * span : d * span + span], ref[...])
        out = term if out is None else out + term
    z = out[:rank] + out[rank:]
    width = z_ref.shape[2]
    for k in range(z_ref.shape[0]):
        part = z[:, k * width : k * width + width]
        z_ref[k] = part + refs[-3][k] if adds else part


def item_columns(place, start_at, ys, a, total=None, only=None, splits=1, block=1024):
    _, items = a.shape
    rows, span = ys[0].shape
    rank = rows * splits
    count = len(ys) // splits
    width = items // 8
    per = block // width
    grid = items // block // (1 if only is None else 2)
    start = 0 if not only else grid
    in_half = items // block // 2

    def of_items(i, s):
        at = i + start
        core = s[place.shape[0] - 1]
        return (at // in_half + 1 + core) % 2 * in_half + at % in_half

    ins = [pl.BlockSpec((rows, span), lambda i, s: (0, 0), pipeline_mode=pl.Buffered(1))] * len(ys)
    for d in range(count):
        ins.append(pl.BlockSpec((span, block), lambda i, s, d=d: (s[start_at + d], of_items(i, s))))
    args = [*ys, *[a] * count]
    if total is not None:
        ins.append(pl.BlockSpec((per, rank, width), lambda i, s: (i + start, 0, 0)))
        args.append(total)
    return pl.pallas_call(
        lambda *refs: columns_kernel(count, splits, total is not None, *refs),
        out_shape=jax.ShapeDtypeStruct((grid * per, rank, width), f32),
        grid_spec=pltpu.PrefetchScalarGridSpec(
            num_scalar_prefetch=1,
            grid=(grid,),
            in_specs=ins,
            out_specs=pl.BlockSpec((per, rank, width), lambda i, s: (i, 0, 0)),
            scratch_shapes=[pltpu.VMEM((2 * rank, count * span), bf16)],
        ),
        name="item_columns",
    )(place, *args)


def inverse_factor_half(block):
    n = block.shape[0]
    count = n // 8
    tile = (8, n)
    lanes = lax.broadcasted_iota(jnp.int32, tile, 1)
    subs = lax.broadcasted_iota(jnp.int32, tile, 0)
    spread = lambda v: jnp.broadcast_to(v, tile)
    rows = [block[8 * k : 8 * k + 8, :] for k in range(count)]
    out = []
    for p in range(count):
        c = 8 * p
        panel = rows[p]
        mine = [spread(panel[:, c + t : c + t + 1]) for t in range(8)]
        invs, leads, tops, scale = [], [], [], jnp.ones(tile, f32)
        for j in range(8):
            pivot = spread(mine[j][j : j + 1, :])
            inv = 1.0 / pivot
            invs.append(inv)
            scale = jnp.where(subs == j, pivot, scale)
            factor = jnp.where(subs > j, mine[j] * inv, 0.0)
            tops.append([None] * (j + 1) + [spread(mine[t][j : j + 1, :]) for t in range(j + 1, 8)])
            for t in range(j + 1, 8):
                mine[t] = mine[t] - factor * tops[j][t]
            panel = jnp.where((lanes == c + j) & (subs >= j), jnp.where(subs == j, 1.0, 0.0), panel)
            lead = spread(panel[j : j + 1, :])
            panel = panel - factor * lead
            leads.append(jnp.where((lanes > c + j) & (lanes < c + 8), 0.0, lead))
        out.append(jnp.where(lanes <= subs + c, panel, 0.0) * lax.rsqrt(scale))
        cleared = (lanes >= c) & (lanes < c + 8)
        for k in range(p + 1, count):
            his = [spread(rows[k][:, c + t : c + t + 1]) for t in range(8)]
            new = jnp.where(cleared, 0.0, rows[k])
            for j in range(8):
                factor = his[j] * invs[j]
                for t in range(j + 1, 8):
                    his[t] = his[t] - factor * tops[j][t]
                new = new - factor * leads[j]
            rows[k] = new
    return jnp.concatenate(out, axis=0)


def inverse_factor(gram, out, block, firsts, belows):
    h = block.shape[0]
    block[...] = gram[:h, :h]

    def half(i, carry):
        first = inverse_factor_half(block[...])
        below = exact_dot(gram[h:, :h], first, 1, 1)
        firsts[i] = first
        belows[i] = below
        block[...] = gram[h:, h:] - exact_dot(below, below, 1, 1)
        return carry

    lax.fori_loop(0, 2, half, 0)
    out[:h, :h] = firsts[0]
    out[:h, h:] = jnp.zeros((h, h), f32)
    out[h:, :h] = -exact_dot(firsts[1], exact_dot(belows[0], firsts[0], 1, 0), 1, 0)
    out[h:, h:] = firsts[1]


def inverse_factor_near_one(gram, out):
    n = gram.shape[0]
    row = lax.broadcasted_iota(jnp.int32, (n, n), 0)
    column = lax.broadcasted_iota(jnp.int32, (n, n), 1)
    one = jnp.where(row == column, 1.0, 0.0)
    lower = jnp.where(row > column, 1.0, jnp.where(row == column, 0.5, 0.0))
    out[...] = one - lower * (gram[...] - one)

    def more(state):
        return (state[1] > 1e-7) & (state[0] < 6)

    def step(state):
        inverse = out[...]
        residual = exact_dot(exact_dot(inverse, gram[...], 1, 0), inverse, 1, 1) - one
        out[...] = inverse - exact_dot(lower * residual, inverse, 1, 0)
        return state[0] + 1, jnp.sum(residual * residual)

    return lax.while_loop(more, step, (0, jnp.float32(1.0)))[1] <= 1e-7


def factor_scratch(rank):
    h = rank // 2
    return [pltpu.VMEM(shape, f32) for shape in ((rank, rank), (h, h), (2, h, h), (2, h, h))]


def of_ring(own, one, three, two):
    return (own + two) + (one + three)


def mine_of(core_ref, gram):
    h, q = gram.shape[0] // 2, gram.shape[0] // 4
    one = jnp.concatenate([gram[:h, :h], gram[h : h + q, :h]], axis=0)
    two = jnp.concatenate([gram[h:, h:], gram[h + q :, :h]], axis=0)
    return jnp.where(core_ref[0] == 0, one, two)


def packed(rank):
    return jax.ShapeDtypeStruct((rank // 2 + rank // 4, rank // 2), f32)


def grams_kernel(*refs):
    for k, ref in enumerate(refs[:-1]):
        part = ref[...]
        refs[-1][k] = exact_dot(part, part, 1, 1)


def grams_of(*parts):
    rank = parts[0].shape[0]
    return pl.pallas_call(
        grams_kernel,
        out_shape=jax.ShapeDtypeStruct((len(parts), rank, rank), f32),
        in_specs=[vmem] * len(parts),
        out_specs=vmem,
        name="part_grams",
    )(*parts)


def last_grams_kernel(core_ref, own_ref, side_ref, *refs):
    total = None
    for k in range(2):
        part = jnp.concatenate([refs[2 * k][...], refs[2 * k + 1][...]], axis=0)
        half = of_ring(own_ref[k], side_ref[2 * k], side_ref[2 * k + 1], exact_dot(part, part, 1, 1))
        total = half if total is None else total + half
    refs[-1][...] = mine_of(core_ref, total)


def first_gram(core, near, far):
    rank = near[0].shape[0]
    own = grams_of(near[0], far[0])
    sides = grams_of(*near[1:3], *far[1:3])
    return pl.pallas_call(
        last_grams_kernel,
        out_shape=packed(rank),
        in_specs=[smem] + [vmem] * 6,
        out_specs=vmem,
        name="last_grams",
    )(core, own, sides, *near[3:], *far[3:])


def whole_gram(core_ref, mine_ref, other_ref, gram):
    h = gram.shape[0] // 2
    mine, other = mine_ref[...], other_ref[...]
    one = jnp.where(core_ref[0] == 0, mine, other)
    two = jnp.where(core_ref[0] == 0, other, mine)
    below = jnp.concatenate([one[h:], two[h:]], axis=0)
    gram[:h, :h], gram[:h, h:] = one[:h], below.T
    gram[h:, :h], gram[h:, h:] = below, two[:h]


def first_kernel(core_ref, slot_ref, mine_ref, other_ref, *refs):
    parts, (basis_ref, out_ref), (held, grams, sems, gram, inverse) = refs[:10], refs[10:12], refs[12:17]
    scratch = refs[17:]
    rows = parts[3].shape[0]
    places = []
    for k in (0, 4):
        places += [held.at[k], held.at[k + 1], held.at[k + 2], held.at[k + 3, :rows], held.at[k + 3, rows:]]
    copies = [pltpu.make_async_copy(ref, place, sems.at[k]) for k, (ref, place) in enumerate(zip(parts, places))]
    for copy in copies:
        copy.start()
    whole_gram(core_ref, mine_ref, other_ref, gram)
    inverse_factor(gram, inverse, *scratch)
    for copy in copies:
        copy.wait()

    def sweep(k, carry):
        block = exact_dot(inverse[...], held[k], 1, 0)
        basis_ref[slot_ref[k]] = block
        grams[k] = good_dot(block, block, 1, 1)
        return carry

    lax.fori_loop(0, 8, sweep, 0, unroll=4)
    halves = [of_ring(*(grams[h * 4 + k] for k in range(4))) for h in range(2)]
    out_ref[...] = mine_of(core_ref, halves[0] + halves[1])


def first_sweep(core, slots, mine, other, parts):
    rank, width = parts[0].shape
    scratch = [pltpu.VMEM((8, rank, width), f32), pltpu.VMEM((8, rank, rank), f32), pltpu.SemaphoreType.DMA((10,))]
    return pl.pallas_call(
        first_kernel,
        out_shape=(jax.ShapeDtypeStruct((8, rank, width), f32), packed(rank)),
        in_specs=[smem, smem, vmem, vmem] + [hbm] * 10,
        out_specs=(vmem, vmem),
        scratch_shapes=scratch + [pltpu.VMEM((rank, rank), f32)] + factor_scratch(rank),
        name="first_sweep",
    )(core, slots, mine, other, *parts)


def second_kernel(scale, core_ref, mine_ref, other_ref, basis_ref, out_ref, gram, inverse, *scratch):
    @pl.when(pl.program_id(0) == 0)
    def _():
        whole_gram(core_ref, mine_ref, other_ref, gram)
        converged = inverse_factor_near_one(gram, inverse)

        @pl.when(jnp.logical_not(converged))
        def _():
            inverse_factor(gram, inverse, *scratch)

    width = basis_ref.shape[2]
    for k in range(basis_ref.shape[0]):
        out_ref[k * width : k * width + width] = good_dot(basis_ref[k], inverse[...], 0, 1) * scale


def second_sweep(core, mine, other, basis, scale, per=2):
    count, rank, width = basis.shape
    return pl.pallas_call(
        lambda *refs: second_kernel(scale, *refs),
        out_shape=jax.ShapeDtypeStruct((count * width, rank), f32),
        grid=(count // per,),
        in_specs=[smem, vmem, vmem, pl.BlockSpec((per, rank, width), lambda i: (i, 0, 0))],
        out_specs=pl.BlockSpec((per * width, rank), lambda i: (i, 0)),
        scratch_shapes=[pltpu.VMEM((rank, rank), f32)] + factor_scratch(rank),
        name="second_sweep",
    )(core, mine, other, basis)


def program(interactions, omega):
    user = lax.axis_index("user")
    z, core, x, y = lax.axis_index("item"), user % 2, user // 2 % side, user // (2 * side)
    a = jnp.where(core == 0, x, y)
    b = jnp.where(core == 0, y, x)
    item_count = omega.shape[0] * lax.axis_size("item")
    width = omega.shape[0] // 8
    from_ring = lambda v, axis: [v] + [shift(v, axis, d) for d in steps]

    place = jnp.stack([*((z + k) % side for k in (2, 1, 3, 0, 3, 1, 2)), core]).astype(jnp.int32)
    offsets = jnp.asarray((0, *steps))
    slots = jnp.concatenate([core * side + (a - offsets) % side, (1 - core) * side + (b - offsets) % side])

    (two,) = user_rows(place, 0, 1, interactions, omega)
    two = shift(two, "item", 2)
    one, three = user_rows(place, 1, 2, interactions, omega)
    one, three = shift(one, "item", 1), shift(three, "item", 3)
    (own,) = user_rows(place, 3, 1, interactions, omega)
    own = of_ring(own, one, three, two)
    one, three = shift(own, "item", 1), shift(own, "item", 3)
    half = own.shape[0] // 2
    two = [shift(one[:half], "item", 1), shift(three[half:], "item", 3)]

    total = item_columns(place, 3, [own], interactions)
    total = item_columns(place, 4, [one, three], interactions, total)
    away = shift(item_columns(place, 6, two, interactions, total, 0, 2), "core")
    kept = item_columns(place, 6, two, interactions, total, 1, 2)

    def block_at(d, halves):
        return sum(lax.dynamic_index_in_dim(h, (a + d) % side, 0, False) for h in halves)

    two = block_at(2, (kept, away))
    two, *halves = lax.optimization_barrier((two, kept, away))
    two = shift(two, "first", 2)
    one, three = block_at(1, halves), block_at(3, halves)
    block = of_ring(block_at(0, halves), shift(one, "first", 1), shift(three, "first", 3), two)
    own_omega = lax.dynamic_slice_in_dim(omega, (core * side + a) * width, width, 0)
    block = of_ring(*from_ring(block, "second")) + ridge * own_omega.T

    half = block.shape[0] // 2
    one, three = shift(block, "first", 1), shift(block, "first", 3)
    near = [block, one, three, shift(one[:half], "first", 1), shift(three[half:], "first", 3)]
    far = [shift(part, "core") for part in near]
    flag = core.reshape(1).astype(jnp.int32)

    def over_items(mine):
        mine = of_ring(*from_ring(mine, "item"))
        return mine, shift(mine, "core")

    basis, gram = first_sweep(flag, slots.astype(jnp.int32), *over_items(first_gram(flag, near, far)), [*near, *far])
    return second_sweep(flag, *over_items(gram), basis, float(item_count) ** 0.5)


def solution(mesh):
    in_specs = (P("user", "item"), P("item", None))
    out_specs = P("item", None)
    return jax.shard_map(program, mesh=mesh, in_specs=in_specs, out_specs=out_specs, check_vma=False)
```

```python
import jax
import jax.numpy as jnp
from jax import lax
from jax.experimental import pallas as pl
from jax.experimental.pallas import tpu as pltpu
from jax.sharding import PartitionSpec as P


ridge = 200.0
highest = lax.Precision.HIGHEST
f32 = jnp.float32
bf16 = jnp.bfloat16
side = 4
steps = (1, 3, 2)


def exact_dot(a, b, ca, cb):
    return lax.dot_general(a, b, (((ca,), (cb,)), ((), ())), precision=highest, preferred_element_type=f32)


def fast_dot(a, b):
    return lax.dot_general(a, b, (((1,), (0,)), ((), ())), preferred_element_type=f32)


def good_dot(a, b, ca, cb):
    dims = (((ca,), (cb,)), ((), ()))
    dot = lambda l, r: lax.dot_general(l, r, dims, preferred_element_type=f32)
    (a0, a1), (b0, b1) = slices(a), slices(b)
    return dot(a0, b0) + (dot(a0, b1) + dot(a1, b0))


def slices(x):
    high = x.astype(bf16)
    return high, (x - high.astype(f32)).astype(bf16)


def pairs_of(axis, step):
    pairs = []
    for u in range(2 * side * side):
        y, x, core = u // (2 * side), u // 2 % side, u % 2
        if axis == "core":
            core = 1 - core
        elif (axis == "first") == (core == 0):
            x = (x + step) % side
        else:
            y = (y + step) % side
        pairs.append((u, (y * side + x) * 2 + core))
    return pairs


def shift(a, axis, step=1):
    if axis == "item":
        return lax.ppermute(a, "item", [(i, (i + step) % side) for i in range(side)])
    return lax.ppermute(a, "user", pairs_of(axis, step))


vmem = pl.BlockSpec(memory_space=pltpu.VMEM)
smem = pl.BlockSpec(memory_space=pltpu.SMEM)
hbm = pl.BlockSpec(memory_space=pl.ANY)


def room(mib):
    return pltpu.CompilerParams(vmem_limit_bytes=mib << 20)


def rows_kernel(count, place_ref, *refs):
    quarters, omega_ref, outs, total = refs[:count], refs[count], refs[count + 1 : -1], refs[-1]
    at, last = pl.program_id(0), pl.num_programs(0) - 1
    span = quarters[0].shape[0]
    high, low = slices(omega_ref[...])
    a = jnp.concatenate([ref[...] for ref in quarters], axis=0)
    y = fast_dot(a, high) + fast_dot(a, low)

    @pl.when(at == 0)
    def _():
        total[...] = y

    @pl.when((at > 0) & (at < last))
    def _():
        total[...] += y

    @pl.when(at == last)
    def _():
        whole = total[...] + y
        for d, out in enumerate(outs):
            out[...] = whole[d * span : d * span + span].T


def user_rows(place, at, count, a, omega, depth=1024):
    users, items = a.shape
    rank = omega.shape[1]
    span = users // side
    return pl.pallas_call(
        lambda *refs: rows_kernel(count, *refs),
        out_shape=(jax.ShapeDtypeStruct((rank, span), f32),) * count,
        grid_spec=pltpu.PrefetchScalarGridSpec(
            num_scalar_prefetch=1,
            grid=(items // depth,),
            in_specs=[pl.BlockSpec((span, depth), lambda k, s, d=d: (s[at + d], k)) for d in range(count)]
            + [pl.BlockSpec((depth, rank), lambda k, s: (k, 0))],
            out_specs=(pl.BlockSpec((rank, span), lambda k, s: (0, 0)),) * count,
            scratch_shapes=[pltpu.VMEM((count * span, rank), f32)],
        ),
        name="user_rows",
        compiler_params=room(50),
    )(place, *[a] * count, omega)


def columns_kernel(count, splits, adds, place_ref, *refs):
    ys, blocks = refs[: count * splits], refs[count * splits : count * splits + count]
    z_ref, both = refs[-2], refs[-1]
    rows, span = ys[0].shape
    rank = rows * splits

    @pl.when(pl.program_id(0) == 0)
    def _():
        for d, ref in enumerate(ys):
            at = slice(d // splits * span, d // splits * span + span)
            row = d % splits * rows
            both[row : row + rows, at], both[rank + row : rank + row + rows, at] = slices(ref[...])

    out = None
    for d, ref in enumerate(blocks):
        term = fast_dot(both[:, d * span : d * span + span], ref[...])
        out = term if out is None else out + term
    z = out[:rank] + out[rank:]
    width = z_ref.shape[2]
    for k in range(z_ref.shape[0]):
        part = z[:, k * width : k * width + width]
        z_ref[k] = part + refs[-3][k] if adds else part


def item_columns(place, start_at, ys, a, total=None, only=None, splits=1, block=1024):
    _, items = a.shape
    rows, span = ys[0].shape
    rank = rows * splits
    count = len(ys) // splits
    width = items // 8
    per = block // width
    grid = items // block // (1 if only is None else 2)
    start = 0 if not only else grid
    in_half = items // block // 2

    def of_items(i, s):
        at = i + start
        core = s[place.shape[0] - 1]
        return (at // in_half + 1 + core) % 2 * in_half + at % in_half

    ins = [pl.BlockSpec((rows, span), lambda i, s: (0, 0), pipeline_mode=pl.Buffered(1))] * len(ys)
    for d in range(count):
        ins.append(pl.BlockSpec((span, block), lambda i, s, d=d: (s[start_at + d], of_items(i, s))))
    args = [*ys, *[a] * count]
    if total is not None:
        ins.append(pl.BlockSpec((per, rank, width), lambda i, s: (i + start, 0, 0)))
        args.append(total)
    return pl.pallas_call(
        lambda *refs: columns_kernel(count, splits, total is not None, *refs),
        out_shape=jax.ShapeDtypeStruct((grid * per, rank, width), f32),
        grid_spec=pltpu.PrefetchScalarGridSpec(
            num_scalar_prefetch=1,
            grid=(grid,),
            in_specs=ins,
            out_specs=pl.BlockSpec((per, rank, width), lambda i, s: (i, 0, 0)),
            scratch_shapes=[pltpu.VMEM((2 * rank, count * span), bf16)],
        ),
        name="item_columns",
        compiler_params=room(44),
    )(place, *args)


def inverse_factor_half(block):
    n = block.shape[0]
    count = n // 8
    tile = (8, n)
    lanes = lax.broadcasted_iota(jnp.int32, tile, 1)
    subs = lax.broadcasted_iota(jnp.int32, tile, 0)
    spread = lambda v: jnp.broadcast_to(v, tile)
    rows = [block[8 * k : 8 * k + 8, :] for k in range(count)]
    out = []
    for p in range(count):
        c = 8 * p
        panel = rows[p]
        mine = [spread(panel[:, c + t : c + t + 1]) for t in range(8)]
        invs, leads, tops, scale = [], [], [], jnp.ones(tile, f32)
        for j in range(8):
            pivot = spread(mine[j][j : j + 1, :])
            inv = 1.0 / pivot
            invs.append(inv)
            scale = jnp.where(subs == j, pivot, scale)
            factor = jnp.where(subs > j, mine[j] * inv, 0.0)
            tops.append([None] * (j + 1) + [spread(mine[t][j : j + 1, :]) for t in range(j + 1, 8)])
            for t in range(j + 1, 8):
                mine[t] = mine[t] - factor * tops[j][t]
            panel = jnp.where((lanes == c + j) & (subs >= j), jnp.where(subs == j, 1.0, 0.0), panel)
            lead = spread(panel[j : j + 1, :])
            panel = panel - factor * lead
            leads.append(jnp.where((lanes > c + j) & (lanes < c + 8), 0.0, lead))
        out.append(jnp.where(lanes <= subs + c, panel, 0.0) * lax.rsqrt(scale))
        cleared = (lanes >= c) & (lanes < c + 8)
        for k in range(p + 1, count):
            his = [spread(rows[k][:, c + t : c + t + 1]) for t in range(8)]
            new = jnp.where(cleared, 0.0, rows[k])
            for j in range(8):
                factor = his[j] * invs[j]
                for t in range(j + 1, 8):
                    his[t] = his[t] - factor * tops[j][t]
                new = new - factor * leads[j]
            rows[k] = new
    return jnp.concatenate(out, axis=0)


def inverse_factor(gram, out, block, firsts, belows):
    h = block.shape[0]
    block[...] = gram[:h, :h]

    def half(i, carry):
        first = inverse_factor_half(block[...])
        below = exact_dot(gram[h:, :h], first, 1, 1)
        firsts[i] = first
        belows[i] = below
        block[...] = gram[h:, h:] - exact_dot(below, below, 1, 1)
        return carry

    lax.fori_loop(0, 2, half, 0)
    out[:h, :h] = firsts[0]
    out[:h, h:] = jnp.zeros((h, h), f32)
    out[h:, :h] = -exact_dot(firsts[1], exact_dot(belows[0], firsts[0], 1, 0), 1, 0)
    out[h:, h:] = firsts[1]


def inverse_factor_near_one(gram, out):
    n = gram.shape[0]
    row = lax.broadcasted_iota(jnp.int32, (n, n), 0)
    column = lax.broadcasted_iota(jnp.int32, (n, n), 1)
    one = jnp.where(row == column, 1.0, 0.0)
    lower = jnp.where(row > column, 1.0, jnp.where(row == column, 0.5, 0.0))
    out[...] = one - lower * (gram[...] - one)

    def more(state):
        return (state[1] > 1e-7) & (state[0] < 6)

    def step(state):
        inverse = out[...]
        residual = exact_dot(exact_dot(inverse, gram[...], 1, 0), inverse, 1, 1) - one
        out[...] = inverse - exact_dot(lower * residual, inverse, 1, 0)
        return state[0] + 1, jnp.sum(residual * residual)

    return lax.while_loop(more, step, (0, jnp.float32(1.0)))[1] <= 1e-7


def factor_scratch(rank):
    h = rank // 2
    return [pltpu.VMEM(shape, f32) for shape in ((rank, rank), (h, h), (2, h, h), (2, h, h))]


def of_ring(own, one, three, two):
    return (own + two) + (one + three)


def mine_of(core_ref, gram):
    h, q = gram.shape[0] // 2, gram.shape[0] // 4
    one = jnp.concatenate([gram[:h, :h], gram[h : h + q, :h]], axis=0)
    two = jnp.concatenate([gram[h:, h:], gram[h + q :, :h]], axis=0)
    return jnp.where(core_ref[0] == 0, one, two)


def packed(rank):
    return jax.ShapeDtypeStruct((rank // 2 + rank // 4, rank // 2), f32)


def grams_kernel(*refs):
    for k, ref in enumerate(refs[:-1]):
        part = ref[...]
        refs[-1][k] = exact_dot(part, part, 1, 1)


def grams_of(*parts):
    rank = parts[0].shape[0]
    return pl.pallas_call(
        grams_kernel,
        out_shape=jax.ShapeDtypeStruct((len(parts), rank, rank), f32),
        in_specs=[vmem] * len(parts),
        out_specs=vmem,
        name="part_grams",
        compiler_params=room(24),
    )(*parts)


def last_grams_kernel(core_ref, own_ref, side_ref, *refs):
    total = None
    for k in range(2):
        part = jnp.concatenate([refs[2 * k][...], refs[2 * k + 1][...]], axis=0)
        half = of_ring(own_ref[k], side_ref[2 * k], side_ref[2 * k + 1], exact_dot(part, part, 1, 1))
        total = half if total is None else total + half
    refs[-1][...] = mine_of(core_ref, total)


def first_gram(core, near, far):
    rank = near[0].shape[0]
    own = grams_of(near[0], far[0])
    sides = grams_of(*near[1:3], *far[1:3])
    return pl.pallas_call(
        last_grams_kernel,
        out_shape=packed(rank),
        in_specs=[smem] + [vmem] * 6,
        out_specs=vmem,
        name="last_grams",
        compiler_params=room(24),
    )(core, own, sides, *near[3:], *far[3:])


def whole_gram(core_ref, mine_ref, other_ref, gram):
    h = gram.shape[0] // 2
    mine, other = mine_ref[...], other_ref[...]
    one = jnp.where(core_ref[0] == 0, mine, other)
    two = jnp.where(core_ref[0] == 0, other, mine)
    below = jnp.concatenate([one[h:], two[h:]], axis=0)
    gram[:h, :h], gram[:h, h:] = one[:h], below.T
    gram[h:, :h], gram[h:, h:] = below, two[:h]


def first_kernel(core_ref, slot_ref, mine_ref, other_ref, *refs):
    parts, (basis_ref, out_ref), (held, grams, sems, gram, inverse) = refs[:10], refs[10:12], refs[12:17]
    scratch = refs[17:]
    rows = parts[3].shape[0]
    places = []
    for k in (0, 4):
        places += [held.at[k], held.at[k + 1], held.at[k + 2], held.at[k + 3, :rows], held.at[k + 3, rows:]]
    copies = [pltpu.make_async_copy(ref, place, sems.at[k]) for k, (ref, place) in enumerate(zip(parts, places))]
    for copy in copies:
        copy.start()
    whole_gram(core_ref, mine_ref, other_ref, gram)
    inverse_factor(gram, inverse, *scratch)
    for copy in copies:
        copy.wait()

    def sweep(k, carry):
        block = exact_dot(inverse[...], held[k], 1, 0)
        basis_ref[slot_ref[k]] = block
        grams[k] = good_dot(block, block, 1, 1)
        return carry

    lax.fori_loop(0, 8, sweep, 0, unroll=4)
    halves = [of_ring(*(grams[h * 4 + k] for k in range(4))) for h in range(2)]
    out_ref[...] = mine_of(core_ref, halves[0] + halves[1])


def first_sweep(core, slots, mine, other, parts):
    rank, width = parts[0].shape
    scratch = [pltpu.VMEM((8, rank, width), f32), pltpu.VMEM((8, rank, rank), f32), pltpu.SemaphoreType.DMA((10,))]
    return pl.pallas_call(
        first_kernel,
        out_shape=(jax.ShapeDtypeStruct((8, rank, width), f32), packed(rank)),
        in_specs=[smem, smem, vmem, vmem] + [hbm] * 10,
        out_specs=(vmem, vmem),
        scratch_shapes=scratch + [pltpu.VMEM((rank, rank), f32)] + factor_scratch(rank),
        name="first_sweep",
        compiler_params=room(32),
    )(core, slots, mine, other, *parts)


def second_kernel(scale, core_ref, mine_ref, other_ref, basis_ref, out_ref, gram, inverse, *scratch):
    @pl.when(pl.program_id(0) == 0)
    def _():
        whole_gram(core_ref, mine_ref, other_ref, gram)
        converged = inverse_factor_near_one(gram, inverse)

        @pl.when(jnp.logical_not(converged))
        def _():
            inverse_factor(gram, inverse, *scratch)

    width = basis_ref.shape[2]
    for k in range(basis_ref.shape[0]):
        out_ref[k * width : k * width + width] = good_dot(basis_ref[k], inverse[...], 0, 1) * scale


def second_sweep(core, mine, other, basis, scale, per=2):
    count, rank, width = basis.shape
    return pl.pallas_call(
        lambda *refs: second_kernel(scale, *refs),
        out_shape=jax.ShapeDtypeStruct((count * width, rank), f32),
        grid=(count // per,),
        in_specs=[smem, vmem, vmem, pl.BlockSpec((per, rank, width), lambda i: (i, 0, 0))],
        out_specs=pl.BlockSpec((per * width, rank), lambda i: (i, 0)),
        scratch_shapes=[pltpu.VMEM((rank, rank), f32)] + factor_scratch(rank),
        name="second_sweep",
        compiler_params=room(32),
    )(core, mine, other, basis)


def program(interactions, omega):
    user = lax.axis_index("user")
    z, core, x, y = lax.axis_index("item"), user % 2, user // 2 % side, user // (2 * side)
    a = jnp.where(core == 0, x, y)
    b = jnp.where(core == 0, y, x)
    item_count = omega.shape[0] * lax.axis_size("item")
    width = omega.shape[0] // 8
    from_ring = lambda v, axis: [v] + [shift(v, axis, d) for d in steps]

    place = jnp.stack([*((z + k) % side for k in (2, 1, 3, 0, 3, 1, 2)), core]).astype(jnp.int32)
    offsets = jnp.asarray((0, *steps))
    slots = jnp.concatenate([core * side + (a - offsets) % side, (1 - core) * side + (b - offsets) % side])

    (two,) = user_rows(place, 0, 1, interactions, omega)
    two = shift(two, "item", 2)
    one, three = user_rows(place, 1, 2, interactions, omega)
    one, three = shift(one, "item", 1), shift(three, "item", 3)
    (own,) = user_rows(place, 3, 1, interactions, omega)
    own = of_ring(own, one, three, two)
    one, three = shift(own, "item", 1), shift(own, "item", 3)
    half = own.shape[0] // 2
    two = [shift(one[:half], "item", 1), shift(three[half:], "item", 3)]

    total = item_columns(place, 3, [own], interactions)
    total = item_columns(place, 4, [one, three], interactions, total)
    away = shift(item_columns(place, 6, two, interactions, total, 0, 2), "core")
    kept = item_columns(place, 6, two, interactions, total, 1, 2)

    def block_at(d, halves):
        return sum(lax.dynamic_index_in_dim(h, (a + d) % side, 0, False) for h in halves)

    two = block_at(2, (kept, away))
    two, *halves = lax.optimization_barrier((two, kept, away))
    two = shift(two, "first", 2)
    one, three = block_at(1, halves), block_at(3, halves)
    block = of_ring(block_at(0, halves), shift(one, "first", 1), shift(three, "first", 3), two)
    own_omega = lax.dynamic_slice_in_dim(omega, (core * side + a) * width, width, 0)
    block = of_ring(*from_ring(block, "second")) + ridge * own_omega.T

    half = block.shape[0] // 2
    one, three = shift(block, "first", 1), shift(block, "first", 3)
    near = [block, one, three, shift(one[:half], "first", 1), shift(three[half:], "first", 3)]
    far = [shift(part, "core") for part in near]
    flag = core.reshape(1).astype(jnp.int32)

    def over_items(mine):
        mine = of_ring(*from_ring(mine, "item"))
        return mine, shift(mine, "core")

    basis, gram = first_sweep(flag, slots.astype(jnp.int32), *over_items(first_gram(flag, near, far)), [*near, *far])
    return second_sweep(flag, *over_items(gram), basis, float(item_count) ** 0.5)


def solution(mesh):
    in_specs = (P("user", "item"), P("item", None))
    out_specs = P("item", None)
    return jax.shard_map(program, mesh=mesh, in_specs=in_specs, out_specs=out_specs, check_vma=False)
```

```python
import jax
import jax.numpy as jnp
from jax import lax
from jax.experimental import pallas as pl
from jax.experimental.pallas import tpu as pltpu
from jax.sharding import PartitionSpec as P


ridge = 200.0
highest = lax.Precision.HIGHEST
f32 = jnp.float32
bf16 = jnp.bfloat16
side = 4
steps = (1, 3, 2)


def exact_dot(a, b, ca, cb):
    return lax.dot_general(a, b, (((ca,), (cb,)), ((), ())), precision=highest, preferred_element_type=f32)


def fast_dot(a, b):
    return lax.dot_general(a, b, (((1,), (0,)), ((), ())), preferred_element_type=f32)


def good_dot(a, b, ca, cb):
    dims = (((ca,), (cb,)), ((), ()))
    dot = lambda l, r: lax.dot_general(l, r, dims, preferred_element_type=f32)
    (a0, a1), (b0, b1) = slices(a), slices(b)
    return dot(a0, b0) + (dot(a0, b1) + dot(a1, b0))


def slices(x):
    high = x.astype(bf16)
    return high, (x - high.astype(f32)).astype(bf16)


def pairs_of(axis, step):
    pairs = []
    for u in range(2 * side * side):
        y, x, core = u // (2 * side), u // 2 % side, u % 2
        if axis == "core":
            core = 1 - core
        elif (axis == "first") == (core == 0):
            x = (x + step) % side
        else:
            y = (y + step) % side
        pairs.append((u, (y * side + x) * 2 + core))
    return pairs


def shift(a, axis, step=1):
    if axis == "item":
        return lax.ppermute(a, "item", [(i, (i + step) % side) for i in range(side)])
    return lax.ppermute(a, "user", pairs_of(axis, step))


vmem = pl.BlockSpec(memory_space=pltpu.VMEM)
smem = pl.BlockSpec(memory_space=pltpu.SMEM)
hbm = pl.BlockSpec(memory_space=pl.ANY)


def room(mib):
    return pltpu.CompilerParams(vmem_limit_bytes=mib << 20)


def rows_kernel(count, place_ref, *refs):
    quarters, omega_ref, outs, total = refs[:count], refs[count], refs[count + 1 : -1], refs[-1]
    at, last = pl.program_id(0), pl.num_programs(0) - 1
    span = quarters[0].shape[0]
    high, low = slices(omega_ref[...])
    a = jnp.concatenate([ref[...] for ref in quarters], axis=0)
    y = fast_dot(a, high) + fast_dot(a, low)

    @pl.when(at == 0)
    def _():
        total[...] = y

    @pl.when((at > 0) & (at < last))
    def _():
        total[...] += y

    @pl.when(at == last)
    def _():
        whole = total[...] + y
        for d, out in enumerate(outs):
            out[...] = whole[d * span : d * span + span].T


def user_rows(place, at, count, a, omega, depth=1024):
    users, items = a.shape
    rank = omega.shape[1]
    span = users // side
    return pl.pallas_call(
        lambda *refs: rows_kernel(count, *refs),
        out_shape=(jax.ShapeDtypeStruct((rank, span), f32),) * count,
        grid_spec=pltpu.PrefetchScalarGridSpec(
            num_scalar_prefetch=1,
            grid=(items // depth,),
            in_specs=[pl.BlockSpec((span, depth), lambda k, s, d=d: (s[at + d], k)) for d in range(count)]
            + [pl.BlockSpec((depth, rank), lambda k, s: (k, 0))],
            out_specs=(pl.BlockSpec((rank, span), lambda k, s: (0, 0)),) * count,
            scratch_shapes=[pltpu.VMEM((count * span, rank), f32)],
        ),
        name="user_rows",
        compiler_params=room(50),
    )(place, *[a] * count, omega)


def columns_kernel(count, splits, adds, place_ref, *refs):
    ys, blocks = refs[: count * splits], refs[count * splits : count * splits + count]
    outs, both = refs[count * splits + count + adds : -1], refs[-1]
    rows, span = ys[0].shape
    rank = rows * splits

    @pl.when(pl.program_id(0) == 0)
    def _():
        for d, ref in enumerate(ys):
            at = slice(d // splits * span, d // splits * span + span)
            row = d % splits * rows
            both[row : row + rows, at], both[rank + row : rank + row + rows, at] = slices(ref[...])

    total = None
    for d, ref in enumerate(blocks):
        term = fast_dot(both[:, d * span : d * span + span], ref[...])
        total = term if total is None else total + term
    z = total[:rank] + total[rank:]
    width = outs[0].shape[2]
    per = pl.num_programs(0) // len(outs)
    for h, out in enumerate(outs):

        @pl.when(pl.program_id(0) // per == h)
        def _():
            for k in range(out.shape[0]):
                part = z[:, k * width : k * width + width]
                out[k] = part + refs[count * splits + count][k] if adds else part


def item_columns(place, at, ys, a, total=None, only=None, parts=1, splits=1, block=1024):
    _, items = a.shape
    rows, span = ys[0].shape
    rank = rows * splits
    count = len(ys) // splits
    width = items // 8
    per = block // width
    grid = items // block // (1 if only is None else 2)
    start = 0 if not only else grid
    in_half = items // block // 2
    of_part = grid // parts

    def of_items(i, s):
        core = s[place.shape[0] - 1]
        return ((i + start) // in_half + 1 + core) % 2 * in_half + (i + start) % in_half

    ins = [pl.BlockSpec((rows, span), lambda i, s: (0, 0), pipeline_mode=pl.Buffered(1))] * len(ys)
    for d in range(count):
        ins.append(pl.BlockSpec((span, block), lambda i, s, d=d: (s[at + d], of_items(i, s))))
    args = [*ys, *[a] * count]
    if total is not None:
        ins.append(pl.BlockSpec((per, rank, width), lambda i, s: (i, 0, 0)))
        args.append(total)
    out = pl.pallas_call(
        lambda *refs: columns_kernel(count, splits, total is not None, *refs),
        out_shape=(jax.ShapeDtypeStruct((of_part * per, rank, width), f32),) * parts,
        grid_spec=pltpu.PrefetchScalarGridSpec(
            num_scalar_prefetch=1,
            grid=(grid,),
            in_specs=ins,
            out_specs=tuple(
                pl.BlockSpec((per, rank, width), lambda i, s, h=h: (jnp.clip(i - h * of_part, 0, of_part - 1), 0, 0))
                for h in range(parts)
            ),
            scratch_shapes=[pltpu.VMEM((2 * rank, count * span), bf16)],
        ),
        name="item_columns",
        compiler_params=room(44),
    )(place, *args)
    return out if parts > 1 else out[0]


def inverse_factor_half(block):
    n = block.shape[0]
    count = n // 8
    tile = (8, n)
    lanes = lax.broadcasted_iota(jnp.int32, tile, 1)
    subs = lax.broadcasted_iota(jnp.int32, tile, 0)
    spread = lambda v: jnp.broadcast_to(v, tile)
    rows = [block[8 * k : 8 * k + 8, :] for k in range(count)]
    out = []
    for p in range(count):
        c = 8 * p
        panel = rows[p]
        mine = [spread(panel[:, c + t : c + t + 1]) for t in range(8)]
        invs, leads, tops, scale = [], [], [], jnp.ones(tile, f32)
        for j in range(8):
            pivot = spread(mine[j][j : j + 1, :])
            inv = 1.0 / pivot
            invs.append(inv)
            scale = jnp.where(subs == j, pivot, scale)
            factor = jnp.where(subs > j, mine[j] * inv, 0.0)
            tops.append([None] * (j + 1) + [spread(mine[t][j : j + 1, :]) for t in range(j + 1, 8)])
            for t in range(j + 1, 8):
                mine[t] = mine[t] - factor * tops[j][t]
            panel = jnp.where((lanes == c + j) & (subs >= j), jnp.where(subs == j, 1.0, 0.0), panel)
            lead = spread(panel[j : j + 1, :])
            panel = panel - factor * lead
            leads.append(jnp.where((lanes > c + j) & (lanes < c + 8), 0.0, lead))
        out.append(jnp.where(lanes <= subs + c, panel, 0.0) * lax.rsqrt(scale))
        cleared = (lanes >= c) & (lanes < c + 8)
        for k in range(p + 1, count):
            his = [spread(rows[k][:, c + t : c + t + 1]) for t in range(8)]
            new = jnp.where(cleared, 0.0, rows[k])
            for j in range(8):
                factor = his[j] * invs[j]
                for t in range(j + 1, 8):
                    his[t] = his[t] - factor * tops[j][t]
                new = new - factor * leads[j]
            rows[k] = new
    return jnp.concatenate(out, axis=0)


def inverse_factor(gram, out, block, firsts, belows):
    h = block.shape[0]
    block[...] = gram[:h, :h]

    def half(i, carry):
        first = inverse_factor_half(block[...])
        below = exact_dot(gram[h:, :h], first, 1, 1)
        firsts[i] = first
        belows[i] = below
        block[...] = gram[h:, h:] - exact_dot(below, below, 1, 1)
        return carry

    lax.fori_loop(0, 2, half, 0)
    out[:h, :h] = firsts[0]
    out[:h, h:] = jnp.zeros((h, h), f32)
    out[h:, :h] = -exact_dot(firsts[1], exact_dot(belows[0], firsts[0], 1, 0), 1, 0)
    out[h:, h:] = firsts[1]


def inverse_factor_near_one(gram, out):
    n = gram.shape[0]
    row = lax.broadcasted_iota(jnp.int32, (n, n), 0)
    column = lax.broadcasted_iota(jnp.int32, (n, n), 1)
    one = jnp.where(row == column, 1.0, 0.0)
    lower = jnp.where(row > column, 1.0, jnp.where(row == column, 0.5, 0.0))
    out[...] = one - lower * (gram[...] - one)

    def more(state):
        return (state[1] > 1e-7) & (state[0] < 6)

    def step(state):
        inverse = out[...]
        residual = exact_dot(exact_dot(inverse, gram[...], 1, 0), inverse, 1, 1) - one
        out[...] = inverse - exact_dot(lower * residual, inverse, 1, 0)
        return state[0] + 1, jnp.sum(residual * residual)

    return lax.while_loop(more, step, (0, jnp.float32(1.0)))[1] <= 1e-7


def factor_scratch(rank):
    h = rank // 2
    return [pltpu.VMEM(shape, f32) for shape in ((rank, rank), (h, h), (2, h, h), (2, h, h))]


def of_ring(own, one, three, two):
    return (own + two) + (one + three)


def mine_of(core_ref, gram):
    h, q = gram.shape[0] // 2, gram.shape[0] // 4
    one = jnp.concatenate([gram[:h, :h], gram[h : h + q, :h]], axis=0)
    two = jnp.concatenate([gram[h:, h:], gram[h + q :, :h]], axis=0)
    return jnp.where(core_ref[0] == 0, one, two)


def packed(rank):
    return jax.ShapeDtypeStruct((rank // 2 + rank // 4, rank // 2), f32)


def grams_kernel(*refs):
    grams = [exact_dot(ref[...], ref[...], 1, 1) for ref in refs[:-1]]
    per = len(grams) // 2
    for k in range(2):
        refs[-1][k] = sum(grams[k * per + 1 : k * per + per], grams[k * per])


def grams_of(near, far):
    rank = near[0].shape[0]
    return pl.pallas_call(
        grams_kernel,
        out_shape=jax.ShapeDtypeStruct((2, rank, rank), f32),
        in_specs=[vmem] * (len(near) + len(far)),
        out_specs=vmem,
        name="part_grams",
        compiler_params=room(24),
    )(*near, *far)


def last_grams_kernel(core_ref, own_ref, side_ref, *refs):
    parts, out_ref, held, sems = refs[:4], refs[4], refs[5], refs[6]
    copies = [pltpu.make_async_copy(ref, held.at[k], sems.at[k]) for k, ref in enumerate((own_ref, side_ref))]
    for copy in copies:
        copy.start()
    lasts = []
    for k in range(2):
        part = jnp.concatenate([parts[2 * k][...], parts[2 * k + 1][...]], axis=0)
        lasts.append(exact_dot(part, part, 1, 1))
    for copy in copies:
        copy.wait()
    halves = [(held[0, k] + lasts[k]) + held[1, k] for k in range(2)]
    out_ref[...] = mine_of(core_ref, halves[0] + halves[1])


def first_gram(core, near, far):
    rank = near[0].shape[0]
    own = grams_of(near[:1], far[:1])
    sides = grams_of(near[1:3], far[1:3])
    return pl.pallas_call(
        last_grams_kernel,
        out_shape=packed(rank),
        in_specs=[smem] + [hbm] * 2 + [vmem] * 4,
        out_specs=vmem,
        scratch_shapes=[pltpu.VMEM((2, 2, rank, rank), f32), pltpu.SemaphoreType.DMA((2,))],
        name="last_grams",
        compiler_params=room(24),
    )(core, own, sides, *near[3:], *far[3:])


def whole_gram(core_ref, mine_ref, other_ref, gram):
    h = gram.shape[0] // 2
    mine, other = mine_ref[...], other_ref[...]
    one = jnp.where(core_ref[0] == 0, mine, other)
    two = jnp.where(core_ref[0] == 0, other, mine)
    below = jnp.concatenate([one[h:], two[h:]], axis=0)
    gram[:h, :h], gram[:h, h:] = one[:h], below.T
    gram[h:, :h], gram[h:, h:] = below, two[:h]


def first_kernel(core_ref, slot_ref, mine_ref, other_ref, *refs):
    parts, (basis_ref, out_ref), (held, grams, sems, gram, inverse) = refs[:10], refs[10:12], refs[12:17]
    scratch = refs[17:]
    rows = parts[3].shape[0]
    places = []
    for k in (0, 4):
        places += [held.at[k], held.at[k + 1], held.at[k + 2], held.at[k + 3, :rows], held.at[k + 3, rows:]]
    copies = [pltpu.make_async_copy(ref, place, sems.at[k]) for k, (ref, place) in enumerate(zip(parts, places))]
    for copy in copies:
        copy.start()
    whole_gram(core_ref, mine_ref, other_ref, gram)
    inverse_factor(gram, inverse, *scratch)
    for copy in copies:
        copy.wait()

    def sweep(k, carry):
        block = exact_dot(inverse[...], held[k], 1, 0)
        basis_ref[slot_ref[k]] = block
        grams[k] = good_dot(block, block, 1, 1)
        return carry

    lax.fori_loop(0, 8, sweep, 0, unroll=4)
    halves = [of_ring(*(grams[h * 4 + k] for k in range(4))) for h in range(2)]
    out_ref[...] = mine_of(core_ref, halves[0] + halves[1])


def first_sweep(core, slots, mine, other, parts):
    rank, width = parts[0].shape
    scratch = [pltpu.VMEM((8, rank, width), f32), pltpu.VMEM((8, rank, rank), f32), pltpu.SemaphoreType.DMA((10,))]
    return pl.pallas_call(
        first_kernel,
        out_shape=(jax.ShapeDtypeStruct((8, rank, width), f32), packed(rank)),
        in_specs=[smem, smem, vmem, vmem] + [hbm] * 10,
        out_specs=(vmem, vmem),
        scratch_shapes=scratch + [pltpu.VMEM((rank, rank), f32)] + factor_scratch(rank),
        name="first_sweep",
        compiler_params=room(32),
    )(core, slots, mine, other, *parts)


def second_kernel(scale, core_ref, mine_ref, other_ref, basis_ref, out_ref, gram, inverse, *scratch):
    @pl.when(pl.program_id(0) == 0)
    def _():
        whole_gram(core_ref, mine_ref, other_ref, gram)
        converged = inverse_factor_near_one(gram, inverse)

        @pl.when(jnp.logical_not(converged))
        def _():
            inverse_factor(gram, inverse, *scratch)

    width = basis_ref.shape[2]
    for k in range(basis_ref.shape[0]):
        out_ref[k * width : k * width + width] = good_dot(basis_ref[k], inverse[...], 0, 1) * scale


def second_sweep(core, mine, other, basis, scale, per=2):
    count, rank, width = basis.shape
    return pl.pallas_call(
        lambda *refs: second_kernel(scale, *refs),
        out_shape=jax.ShapeDtypeStruct((count * width, rank), f32),
        grid=(count // per,),
        in_specs=[smem, vmem, vmem, pl.BlockSpec((per, rank, width), lambda i: (i, 0, 0))],
        out_specs=pl.BlockSpec((per * width, rank), lambda i: (i, 0)),
        scratch_shapes=[pltpu.VMEM((rank, rank), f32)] + factor_scratch(rank),
        name="second_sweep",
        compiler_params=room(32),
    )(core, mine, other, basis)


def program(interactions, omega):
    user = lax.axis_index("user")
    z, core, x, y = lax.axis_index("item"), user % 2, user // 2 % side, user // (2 * side)
    a = jnp.where(core == 0, x, y)
    b = jnp.where(core == 0, y, x)
    item_count = omega.shape[0] * lax.axis_size("item")
    width = omega.shape[0] // 8
    from_ring = lambda v, axis: [v] + [shift(v, axis, d) for d in steps]

    place = jnp.stack([*((z + k) % side for k in (2, 1, 3, 0, 3, 1, 2)), core]).astype(jnp.int32)
    offsets = jnp.asarray((0, *steps))
    slots = jnp.concatenate([core * side + (a - offsets) % side, (1 - core) * side + (b - offsets) % side])

    (two,) = user_rows(place, 0, 1, interactions, omega)
    two = shift(two, "item", 2)
    one, three = user_rows(place, 1, 2, interactions, omega)
    one, three = shift(one, "item", 1), shift(three, "item", 3)
    (own,) = user_rows(place, 3, 1, interactions, omega)
    own = of_ring(own, one, three, two)
    one, three = shift(own, "item", 1), shift(own, "item", 3)
    half = own.shape[0] // 2
    two = [shift(one[:half], "item", 1), shift(three[half:], "item", 3)]

    total = item_columns(place, 3, [own], interactions)
    sent, kept = item_columns(place, 4, [one, three], interactions, total, parts=2)
    away = shift(item_columns(place, 6, two, interactions, sent, 0, splits=2), "core")
    kept = item_columns(place, 6, two, interactions, kept, 1, splits=2)

    def block_at(d, halves):
        return sum(lax.dynamic_index_in_dim(h, (a + d) % side, 0, False) for h in halves)

    two = block_at(2, (kept, away))
    two, *halves = lax.optimization_barrier((two, kept, away))
    two = shift(two, "first", 2)
    one, three = block_at(1, halves), block_at(3, halves)
    one, three, *halves = lax.optimization_barrier((one, three, *halves))
    one, three = shift(one, "first", 1), shift(three, "first", 3)
    block = lax.optimization_barrier(block_at(0, halves))
    block = of_ring(block, one, three, two)
    own_omega = lax.dynamic_slice_in_dim(omega, (core * side + a) * width, width, 0)
    block = of_ring(*from_ring(block, "second")) + ridge * own_omega.T

    half = block.shape[0] // 2
    one, three = shift(block, "first", 1), shift(block, "first", 3)
    near = [block, one, three, shift(one[:half], "first", 1), shift(three[half:], "first", 3)]
    far = [shift(part, "core") for part in near]
    flag = core.reshape(1).astype(jnp.int32)

    def over_items(mine):
        mine = of_ring(*from_ring(mine, "item"))
        return mine, shift(mine, "core")

    basis, gram = first_sweep(flag, slots.astype(jnp.int32), *over_items(first_gram(flag, near, far)), [*near, *far])
    return second_sweep(flag, *over_items(gram), basis, float(item_count) ** 0.5)


def solution(mesh):
    in_specs = (P("user", "item"), P("item", None))
    out_specs = P("item", None)
    return jax.shard_map(program, mesh=mesh, in_specs=in_specs, out_specs=out_specs, check_vma=False)
```

```python
import jax
import jax.numpy as jnp
from jax import lax
from jax.experimental import pallas as pl
from jax.experimental.pallas import tpu as pltpu
from jax.sharding import PartitionSpec as P


ridge = 200.0
highest = lax.Precision.HIGHEST
f32 = jnp.float32
bf16 = jnp.bfloat16
side = 4
steps = (1, 3, 2)


def exact_dot(a, b, ca, cb):
    return lax.dot_general(a, b, (((ca,), (cb,)), ((), ())), precision=highest, preferred_element_type=f32)


def fast_dot(a, b):
    return lax.dot_general(a, b, (((1,), (0,)), ((), ())), preferred_element_type=f32)


def good_dot(a, b, ca, cb):
    dims = (((ca,), (cb,)), ((), ()))
    dot = lambda l, r: lax.dot_general(l, r, dims, preferred_element_type=f32)
    (a0, a1), (b0, b1) = slices(a), slices(b)
    return dot(a0, b0) + (dot(a0, b1) + dot(a1, b0))


def slices(x):
    high = x.astype(bf16)
    return high, (x - high.astype(f32)).astype(bf16)


def pairs_of(axis, step):
    pairs = []
    for u in range(2 * side * side):
        y, x, core = u // (2 * side), u // 2 % side, u % 2
        if axis == "core":
            core = 1 - core
        elif (axis == "first") == (core == 0):
            x = (x + step) % side
        else:
            y = (y + step) % side
        pairs.append((u, (y * side + x) * 2 + core))
    return pairs


def shift(a, axis, step=1):
    if axis == "item":
        return lax.ppermute(a, "item", [(i, (i + step) % side) for i in range(side)])
    return lax.ppermute(a, "user", pairs_of(axis, step))


vmem = pl.BlockSpec(memory_space=pltpu.VMEM)
smem = pl.BlockSpec(memory_space=pltpu.SMEM)
hbm = pl.BlockSpec(memory_space=pl.ANY)


def room(mib):
    return pltpu.CompilerParams(vmem_limit_bytes=mib << 20)


def rows_kernel(count, place_ref, *refs):
    quarters, omega_ref, outs, total = refs[:count], refs[count], refs[count + 1 : -1], refs[-1]
    at, last = pl.program_id(0), pl.num_programs(0) - 1
    span = quarters[0].shape[0]
    high, low = slices(omega_ref[...])
    a = jnp.concatenate([ref[...] for ref in quarters], axis=0)
    y = fast_dot(a, high) + fast_dot(a, low)

    @pl.when(at == 0)
    def _():
        total[...] = y

    @pl.when((at > 0) & (at < last))
    def _():
        total[...] += y

    @pl.when(at == last)
    def _():
        whole = total[...] + y
        for d, out in enumerate(outs):
            out[...] = whole[d * span : d * span + span].T


def user_rows(place, at, count, a, omega, depth=1024):
    users, items = a.shape
    rank = omega.shape[1]
    span = users // side
    return pl.pallas_call(
        lambda *refs: rows_kernel(count, *refs),
        out_shape=(jax.ShapeDtypeStruct((rank, span), f32),) * count,
        grid_spec=pltpu.PrefetchScalarGridSpec(
            num_scalar_prefetch=1,
            grid=(items // depth,),
            in_specs=[pl.BlockSpec((span, depth), lambda k, s, d=d: (s[at + d], k)) for d in range(count)]
            + [pl.BlockSpec((depth, rank), lambda k, s: (k, 0))],
            out_specs=(pl.BlockSpec((rank, span), lambda k, s: (0, 0)),) * count,
            scratch_shapes=[pltpu.VMEM((count * span, rank), f32)],
        ),
        name="user_rows",
        compiler_params=room(50),
    )(place, *[a] * count, omega)


def columns_kernel(count, splits, adds, place_ref, *refs):
    ys, blocks = refs[: count * splits], refs[count * splits : count * splits + count]
    outs, both = refs[count * splits + count + adds : -1], refs[-1]
    rows, span = ys[0].shape
    rank = rows * splits

    @pl.when(pl.program_id(0) == 0)
    def _():
        for d, ref in enumerate(ys):
            at = slice(d // splits * span, d // splits * span + span)
            row = d % splits * rows
            both[row : row + rows, at], both[rank + row : rank + row + rows, at] = slices(ref[...])

    total = None
    for d, ref in enumerate(blocks):
        term = fast_dot(both[:, d * span : d * span + span], ref[...])
        total = term if total is None else total + term
    z = total[:rank] + total[rank:]
    width = outs[0].shape[2]
    per = pl.num_programs(0) // len(outs)
    for h, out in enumerate(outs):

        @pl.when(pl.program_id(0) // per == h)
        def _():
            for k in range(out.shape[0]):
                part = z[:, k * width : k * width + width]
                out[k] = part + refs[count * splits + count][k] if adds else part


def item_columns(place, at, ys, a, total=None, only=None, parts=1, splits=1, block=1024):
    _, items = a.shape
    rows, span = ys[0].shape
    rank = rows * splits
    count = len(ys) // splits
    width = items // 8
    per = block // width
    grid = items // block // (1 if only is None else 2)
    start = 0 if not only else grid
    in_half = items // block // 2
    of_part = grid // parts

    def of_items(i, s):
        core = s[place.shape[0] - 1]
        return ((i + start) // in_half + 1 + core) % 2 * in_half + (i + start) % in_half

    ins = [pl.BlockSpec((rows, span), lambda i, s: (0, 0), pipeline_mode=pl.Buffered(1))] * len(ys)
    for d in range(count):
        ins.append(pl.BlockSpec((span, block), lambda i, s, d=d: (s[at + d], of_items(i, s))))
    args = [*ys, *[a] * count]
    if total is not None:
        ins.append(pl.BlockSpec((per, rank, width), lambda i, s: (i, 0, 0)))
        args.append(total)
    out = pl.pallas_call(
        lambda *refs: columns_kernel(count, splits, total is not None, *refs),
        out_shape=(jax.ShapeDtypeStruct((of_part * per, rank, width), f32),) * parts,
        grid_spec=pltpu.PrefetchScalarGridSpec(
            num_scalar_prefetch=1,
            grid=(grid,),
            in_specs=ins,
            out_specs=tuple(
                pl.BlockSpec((per, rank, width), lambda i, s, h=h: (jnp.clip(i - h * of_part, 0, of_part - 1), 0, 0))
                for h in range(parts)
            ),
            scratch_shapes=[pltpu.VMEM((2 * rank, count * span), bf16)],
        ),
        name="item_columns",
        compiler_params=room(44),
    )(place, *args)
    return out if parts > 1 else out[0]


def inverse_factor_half(block):
    n = block.shape[0]
    count = n // 8
    tile = (8, n)
    lanes = lax.broadcasted_iota(jnp.int32, tile, 1)
    subs = lax.broadcasted_iota(jnp.int32, tile, 0)
    spread = lambda v: jnp.broadcast_to(v, tile)
    rows = [block[8 * k : 8 * k + 8, :] for k in range(count)]
    out = []
    for p in range(count):
        c = 8 * p
        panel = rows[p]
        mine = [spread(panel[:, c + t : c + t + 1]) for t in range(8)]
        invs, leads, tops, scale = [], [], [], jnp.ones(tile, f32)
        for j in range(8):
            pivot = spread(mine[j][j : j + 1, :])
            inv = 1.0 / pivot
            invs.append(inv)
            scale = jnp.where(subs == j, pivot, scale)
            factor = jnp.where(subs > j, mine[j] * inv, 0.0)
            tops.append([None] * (j + 1) + [spread(mine[t][j : j + 1, :]) for t in range(j + 1, 8)])
            for t in range(j + 1, 8):
                mine[t] = mine[t] - factor * tops[j][t]
            panel = jnp.where((lanes == c + j) & (subs >= j), jnp.where(subs == j, 1.0, 0.0), panel)
            lead = spread(panel[j : j + 1, :])
            panel = panel - factor * lead
            leads.append(jnp.where((lanes > c + j) & (lanes < c + 8), 0.0, lead))
        out.append(jnp.where(lanes <= subs + c, panel, 0.0) * lax.rsqrt(scale))
        cleared = (lanes >= c) & (lanes < c + 8)
        for k in range(p + 1, count):
            his = [spread(rows[k][:, c + t : c + t + 1]) for t in range(8)]
            new = jnp.where(cleared, 0.0, rows[k])
            for j in range(8):
                factor = his[j] * invs[j]
                for t in range(j + 1, 8):
                    his[t] = his[t] - factor * tops[j][t]
                new = new - factor * leads[j]
            rows[k] = new
    return jnp.concatenate(out, axis=0)


def inverse_factor(gram, out, block, firsts, belows):
    h = block.shape[0]
    block[...] = gram[:h, :h]

    def half(i, carry):
        first = inverse_factor_half(block[...])
        below = exact_dot(gram[h:, :h], first, 1, 1)
        firsts[i] = first
        belows[i] = below
        block[...] = gram[h:, h:] - exact_dot(below, below, 1, 1)
        return carry

    lax.fori_loop(0, 2, half, 0)
    out[:h, :h] = firsts[0]
    out[:h, h:] = jnp.zeros((h, h), f32)
    out[h:, :h] = -exact_dot(firsts[1], exact_dot(belows[0], firsts[0], 1, 0), 1, 0)
    out[h:, h:] = firsts[1]


def inverse_factor_near_one(gram, out):
    n = gram.shape[0]
    row = lax.broadcasted_iota(jnp.int32, (n, n), 0)
    column = lax.broadcasted_iota(jnp.int32, (n, n), 1)
    one = jnp.where(row == column, 1.0, 0.0)
    lower = jnp.where(row > column, 1.0, jnp.where(row == column, 0.5, 0.0))
    out[...] = one - lower * (gram[...] - one)

    def more(state):
        return (state[1] > 1e-7) & (state[0] < 6)

    def step(state):
        inverse = out[...]
        residual = exact_dot(exact_dot(inverse, gram[...], 1, 0), inverse, 1, 1) - one
        out[...] = inverse - exact_dot(lower * residual, inverse, 1, 0)
        return state[0] + 1, jnp.sum(residual * residual)

    return lax.while_loop(more, step, (0, jnp.float32(1.0)))[1] <= 1e-7


def factor_scratch(rank):
    h = rank // 2
    return [pltpu.VMEM(shape, f32) for shape in ((rank, rank), (h, h), (2, h, h), (2, h, h))]


def of_ring(own, one, three, two):
    return (own + two) + (one + three)


def mine_of(core_ref, gram):
    h, q = gram.shape[0] // 2, gram.shape[0] // 4
    one = jnp.concatenate([gram[:h, :h], gram[h : h + q, :h]], axis=0)
    two = jnp.concatenate([gram[h:, h:], gram[h + q :, :h]], axis=0)
    return jnp.where(core_ref[0] == 0, one, two)


def packed(rank):
    return jax.ShapeDtypeStruct((rank // 2 + rank // 4, rank // 2), f32)


def grams_kernel(*refs):
    grams = [exact_dot(ref[...], ref[...], 1, 1) for ref in refs[:-1]]
    per = len(grams) // 2
    for k in range(2):
        refs[-1][k] = sum(grams[k * per + 1 : k * per + per], grams[k * per])


def grams_of(near, far):
    rank = near[0].shape[0]
    return pl.pallas_call(
        grams_kernel,
        out_shape=jax.ShapeDtypeStruct((2, rank, rank), f32),
        in_specs=[vmem] * (len(near) + len(far)),
        out_specs=vmem,
        name="part_grams",
        compiler_params=room(24),
    )(*near, *far)


def last_grams_kernel(core_ref, own_ref, side_ref, *refs):
    parts, out_ref, held, sems = refs[:4], refs[4], refs[5], refs[6]
    copies = [pltpu.make_async_copy(ref, held.at[k], sems.at[k]) for k, ref in enumerate((own_ref, side_ref))]
    for copy in copies:
        copy.start()
    lasts = []
    for k in range(2):
        part = jnp.concatenate([parts[2 * k][...], parts[2 * k + 1][...]], axis=0)
        lasts.append(exact_dot(part, part, 1, 1))
    for copy in copies:
        copy.wait()
    halves = [(held[0, k] + lasts[k]) + held[1, k] for k in range(2)]
    out_ref[...] = mine_of(core_ref, halves[0] + halves[1])


def first_gram(core, near, far):
    rank = near[0].shape[0]
    own = grams_of(near[:1], far[:1])
    sides = grams_of(near[1:3], far[1:3])
    return pl.pallas_call(
        last_grams_kernel,
        out_shape=packed(rank),
        in_specs=[smem] + [pl.BlockSpec(memory_space=pltpu.HBM)] * 2 + [vmem] * 4,
        out_specs=vmem,
        scratch_shapes=[pltpu.VMEM((2, 2, rank, rank), f32), pltpu.SemaphoreType.DMA((2,))],
        name="last_grams",
        compiler_params=room(24),
    )(core, *(pltpu.with_memory_space_constraint(g, pltpu.HBM) for g in (own, sides)), *near[3:], *far[3:])


def whole_gram(core_ref, mine_ref, other_ref, gram):
    h = gram.shape[0] // 2
    mine, other = mine_ref[...], other_ref[...]
    one = jnp.where(core_ref[0] == 0, mine, other)
    two = jnp.where(core_ref[0] == 0, other, mine)
    below = jnp.concatenate([one[h:], two[h:]], axis=0)
    gram[:h, :h], gram[:h, h:] = one[:h], below.T
    gram[h:, :h], gram[h:, h:] = below, two[:h]


def first_kernel(core_ref, slot_ref, mine_ref, other_ref, *refs):
    parts, (basis_ref, out_ref), (held, grams, sems, gram, inverse) = refs[:10], refs[10:12], refs[12:17]
    scratch = refs[17:]
    rows = parts[3].shape[0]
    places = []
    for k in (0, 4):
        places += [held.at[k], held.at[k + 1], held.at[k + 2], held.at[k + 3, :rows], held.at[k + 3, rows:]]
    copies = [pltpu.make_async_copy(ref, place, sems.at[k]) for k, (ref, place) in enumerate(zip(parts, places))]
    for copy in copies:
        copy.start()
    whole_gram(core_ref, mine_ref, other_ref, gram)
    inverse_factor(gram, inverse, *scratch)
    for copy in copies:
        copy.wait()

    def sweep(k, carry):
        block = exact_dot(inverse[...], held[k], 1, 0)
        basis_ref[slot_ref[k]] = block
        grams[k] = good_dot(block, block, 1, 1)
        return carry

    lax.fori_loop(0, 8, sweep, 0, unroll=4)
    halves = [of_ring(*(grams[h * 4 + k] for k in range(4))) for h in range(2)]
    out_ref[...] = mine_of(core_ref, halves[0] + halves[1])


def first_sweep(core, slots, mine, other, parts):
    rank, width = parts[0].shape
    scratch = [pltpu.VMEM((8, rank, width), f32), pltpu.VMEM((8, rank, rank), f32), pltpu.SemaphoreType.DMA((10,))]
    return pl.pallas_call(
        first_kernel,
        out_shape=(jax.ShapeDtypeStruct((8, rank, width), f32), packed(rank)),
        in_specs=[smem, smem, vmem, vmem] + [hbm] * 10,
        out_specs=(vmem, vmem),
        scratch_shapes=scratch + [pltpu.VMEM((rank, rank), f32)] + factor_scratch(rank),
        name="first_sweep",
        compiler_params=room(32),
    )(core, slots, mine, other, *parts)


def second_kernel(scale, core_ref, mine_ref, other_ref, basis_ref, out_ref, gram, inverse, *scratch):
    @pl.when(pl.program_id(0) == 0)
    def _():
        whole_gram(core_ref, mine_ref, other_ref, gram)
        converged = inverse_factor_near_one(gram, inverse)

        @pl.when(jnp.logical_not(converged))
        def _():
            inverse_factor(gram, inverse, *scratch)

    width = basis_ref.shape[2]
    for k in range(basis_ref.shape[0]):
        out_ref[k * width : k * width + width] = good_dot(basis_ref[k], inverse[...], 0, 1) * scale


def second_sweep(core, mine, other, basis, scale, per=2):
    count, rank, width = basis.shape
    return pl.pallas_call(
        lambda *refs: second_kernel(scale, *refs),
        out_shape=jax.ShapeDtypeStruct((count * width, rank), f32),
        grid=(count // per,),
        in_specs=[smem, vmem, vmem, pl.BlockSpec((per, rank, width), lambda i: (i, 0, 0))],
        out_specs=pl.BlockSpec((per * width, rank), lambda i: (i, 0)),
        scratch_shapes=[pltpu.VMEM((rank, rank), f32)] + factor_scratch(rank),
        name="second_sweep",
        compiler_params=room(32),
    )(core, mine, other, basis)


def program(interactions, omega):
    user = lax.axis_index("user")
    z, core, x, y = lax.axis_index("item"), user % 2, user // 2 % side, user // (2 * side)
    a = jnp.where(core == 0, x, y)
    b = jnp.where(core == 0, y, x)
    item_count = omega.shape[0] * lax.axis_size("item")
    width = omega.shape[0] // 8
    from_ring = lambda v, axis: [v] + [shift(v, axis, d) for d in steps]

    place = jnp.stack([*((z + k) % side for k in (2, 1, 3, 0, 3, 1, 2)), core]).astype(jnp.int32)
    offsets = jnp.asarray((0, *steps))
    slots = jnp.concatenate([core * side + (a - offsets) % side, (1 - core) * side + (b - offsets) % side])

    (two,) = user_rows(place, 0, 1, interactions, omega)
    two = shift(two, "item", 2)
    one, three = user_rows(place, 1, 2, interactions, omega)
    one, three = shift(one, "item", 1), shift(three, "item", 3)
    (own,) = user_rows(place, 3, 1, interactions, omega)
    own = of_ring(own, one, three, two)
    one, three = shift(own, "item", 1), shift(own, "item", 3)
    half = own.shape[0] // 2
    two = [shift(one[:half], "item", 1), shift(three[half:], "item", 3)]

    total = item_columns(place, 3, [own], interactions)
    sent, kept = item_columns(place, 4, [one, three], interactions, total, parts=2)
    away = shift(item_columns(place, 6, two, interactions, sent, 0, splits=2), "core")
    kept = pltpu.with_memory_space_constraint(kept, pltpu.HBM)
    kept = item_columns(place, 6, two, interactions, kept, 1, splits=2)

    def block_at(d, halves):
        return sum(lax.dynamic_index_in_dim(h, (a + d) % side, 0, False) for h in halves)

    two = block_at(2, (kept, away))
    two, *halves = lax.optimization_barrier((two, kept, away))
    two = shift(two, "first", 2)
    one, three = block_at(1, halves), block_at(3, halves)
    block = of_ring(block_at(0, halves), shift(one, "first", 1), shift(three, "first", 3), two)
    own_omega = lax.dynamic_slice_in_dim(omega, (core * side + a) * width, width, 0)
    block = of_ring(*from_ring(block, "second")) + ridge * own_omega.T

    half = block.shape[0] // 2
    one, three = shift(block, "first", 1), shift(block, "first", 3)
    near = [block, one, three, shift(one[:half], "first", 1), shift(three[half:], "first", 3)]
    far = [shift(part, "core") for part in near]
    flag = core.reshape(1).astype(jnp.int32)

    def over_items(mine):
        mine = of_ring(*from_ring(mine, "item"))
        return mine, shift(mine, "core")

    basis, gram = first_sweep(flag, slots.astype(jnp.int32), *over_items(first_gram(flag, near, far)), [*near, *far])
    return second_sweep(flag, *over_items(gram), basis, float(item_count) ** 0.5)


def solution(mesh):
    in_specs = (P("user", "item"), P("item", None))
    out_specs = P("item", None)
    return jax.shard_map(program, mesh=mesh, in_specs=in_specs, out_specs=out_specs, check_vma=False)
```
